32 devices in a mesh: groups: 1, frames: 32 (over z, y, x, core).
Axes of the slice: x: 2, y: 2, z: 4, core: 2. Of those that a mesh axis runs over, the one named last changes fastest.
Arguments:
- skip: bfloat16 [32, 256, 640], P(('groups', 'frames')), may hold values from -24 to 24
- control: bfloat16 [32, 256, 640], P('groups', 'frames'), may hold values from -6 to 6
- zero_weight: bfloat16 [640, 640], replicated, may hold values from -1 to 1
- gn_gain: float32 [640], replicated, may hold values from 0.1 to 1.9
- gn_bias: float32 [640], replicated, may hold values from -0.5 to 0.5
- conv_weight: bfloat16 [9, 640, 640], replicated, may hold values from -0.078125 to 0.078125
- ln_gain: float32 [640], replicated, may hold values from 0.1 to 1.9
- qkv_weight: bfloat16 [640, 1920], replicated, may hold values from -5 to 5
- out_weight: bfloat16 [640, 640], replicated, may hold values from -0.25 to 0.25
Outputs:
- output: bfloat16 [32, 256, 640], P(('groups', 'frames'))
The draws below stay inside these ranges and needn't reach their ends.
All inputs are finite; a program needn't handle non-finite values.
Results may differ from the reference program's by a relative error of at most 0.0043.
Values may be sent and summed in bfloat16 or wider, within the bound.
No kernel may reach another device: no remote copies, remote signals or barrier semaphores. Data moves between devices by JAX's collectives and lax.ppermute only.
A program may use at most 64 MiB of HBM per device.

```python
import math
import jax
import jax.numpy as jnp
from jax import lax

C = 640
HEADS = 10
HD = 64
GROUPS = 32
CLIP = 32
H = 8
W = 32
FRAMES = 32
PIX = 256


def shared_jitter(key):
    jitter = jax.random.uniform(jax.random.fold_in(key, 101), (FRAMES, GROUPS), jnp.float32, -4.0, 4.0)
    return jnp.repeat(jitter, C // GROUPS, axis=1)[:, None, :]


def draw_skip(key, part):
    first_key = jax.random.fold_in(jax.random.fold_in(key, 11), 0)
    fourth_key = jax.random.fold_in(jax.random.fold_in(key, 11), 3)
    fifth_key = jax.random.fold_in(jax.random.fold_in(key, 11), 4)
    frame_pos = (jnp.arange(FRAMES) % CLIP).astype(jnp.float32)
    ramp = (1.0 + 2.0 * frame_pos / (CLIP - 1))[:, None, None]
    magnitude = jax.random.uniform(fourth_key, (GROUPS,), jnp.float32, 0.75, 1.75)
    flips = jnp.where(jax.random.uniform(fifth_key, (GROUPS,), jnp.float32) > 0.5, 1.0, -1.0)
    offset = jnp.repeat(magnitude * flips, C // GROUPS)[None, None, :]
    jitter = shared_jitter(key)
    values = (jnp.clip(jax.random.normal(first_key, (FRAMES, PIX, C), jnp.float32), -6.0, 6.0) + offset) * ramp + jitter
    return jnp.clip(values, -24.0, 24.0).astype(jnp.bfloat16)


def draw_control(key, part):
    first_key, second_key = jax.random.split(jax.random.fold_in(key, 37), 2)
    coupling = jax.random.uniform(first_key, (GROUPS,), jnp.float32, 0.6, 1.4)
    coupling = jnp.repeat(coupling, C // GROUPS)[None, None, :]
    jitter = shared_jitter(key)
    noise = jnp.clip(jax.random.normal(second_key, (FRAMES, PIX, C), jnp.float32), -4.0, 4.0)
    return jnp.clip(coupling * jitter + noise, -6.0, 6.0).astype(jnp.bfloat16)


def draw_zero_weight(key, part):
    noise = jnp.clip(jax.random.normal(jax.random.fold_in(key, 53), (C, C), jnp.float32), -4.0, 4.0)
    values = 0.75 * jnp.eye(C, dtype=jnp.float32) + 0.7 * C ** (-0.5) * noise
    return jnp.clip(values, -1.0, 1.0).astype(jnp.bfloat16)


def draw_qkv_weight(key, part):
    noise = jnp.clip(jax.random.normal(jax.random.fold_in(key, 23), (C, 3 * C), jnp.float32), -6.0, 6.0) * C ** (-0.5)
    return jnp.clip(noise, -5.0, 5.0).astype(jnp.bfloat16)


def normal_values(key, dims, spread, reach, kind=jnp.bfloat16):
    array = spread * jax.random.normal(key, dims, jnp.float32)
    return jnp.clip(array, min=-reach, max=reach).astype(kind)


def setup_inputs(seed: int = 0, part: int = 0) -> dict:
    key_of = jax.random.split(jax.random.key(seed), 10)
    own_keys = jax.random.split(jax.random.fold_in(key_of[9], part), 10)
    skip = draw_skip(jax.random.fold_in(jax.random.fold_in(key_of[9], part), 71), part)
    control = draw_control(jax.random.fold_in(jax.random.fold_in(key_of[9], part), 71), part)
    zero_weight = draw_zero_weight(jax.random.fold_in(key_of[9], 71), part)
    gn_gain = jnp.clip(1.0 + 0.18 * jax.random.normal(key_of[3], (C,), jnp.float32), 0.1, 1.9)
    gn_bias = jnp.clip(jax.random.uniform(key_of[4], (C,), jnp.float32, -0.5, 0.5), -0.5, 0.5)
    conv_weight = normal_values(key_of[5], (9, C, C), (9 * C) ** -0.5, 0.078125)
    ln_gain = jnp.clip(1.0 + 0.18 * jax.random.normal(key_of[6], (C,), jnp.float32), 0.1, 1.9)
    qkv_weight = draw_qkv_weight(jax.random.fold_in(key_of[9], 71), part)
    out_weight = normal_values(key_of[8], (C, C), C ** -0.5, 0.25)
    return {"skip": skip, "control": control, "zero_weight": zero_weight, "gn_gain": gn_gain, "gn_bias": gn_bias, "conv_weight": conv_weight, "ln_gain": ln_gain, "qkv_weight": qkv_weight, "out_weight": out_weight}


norm_epsilon = 1e-05

def attend_all(qkv_rows):
    frame_count, pixel_count, _ = qkv_rows.shape
    clip_count = frame_count // CLIP
    shaped = qkv_rows.astype(jnp.float32).reshape(clip_count, CLIP, pixel_count, 3, HEADS, HD)
    queries = shaped[:, :, :, 0]
    key_rows = shaped[:, :, :, 1]
    value_rows = shaped[:, :, :, 2]
    scores = jnp.einsum('atphd,asphd->aphts', queries, key_rows, precision=lax.Precision.HIGHEST) * (1.0 / math.sqrt(HD))
    scores = scores - lax.optimization_barrier(jnp.max(scores, axis=-1, keepdims=True))
    expon = jnp.exp(scores)
    attn_weights = (expon / lax.optimization_barrier(jnp.sum(expon, axis=-1, keepdims=True))).astype(jnp.bfloat16)
    mixed = jnp.einsum('aphts,asphd->atphd', attn_weights.astype(jnp.float32), value_rows, precision=lax.Precision.HIGHEST)
    return mixed.astype(jnp.bfloat16).reshape(frame_count, pixel_count, C)

def reference(skip, control, zero_weight, gn_gain, gn_bias, conv_weight, ln_gain, qkv_weight, out_weight):
    zero_out = jnp.dot(control.reshape(-1, C), zero_weight, preferred_element_type=jnp.float32).astype(jnp.bfloat16)
    joined = skip.astype(jnp.float32) + zero_out.reshape(FRAMES, PIX, C).astype(jnp.float32)
    grouped = joined.reshape(FRAMES // CLIP, CLIP, PIX, GROUPS, C // GROUPS)
    clip_mean = lax.optimization_barrier(jnp.mean(grouped, axis=(1, 2, 4), keepdims=True))
    clip_var = lax.optimization_barrier(jnp.mean(jnp.square(grouped - clip_mean), axis=(1, 2, 4), keepdims=True))
    normed_groups = ((grouped - clip_mean) * lax.rsqrt(clip_var + norm_epsilon)).reshape(FRAMES, PIX, C)
    activated = jax.nn.silu(normed_groups * gn_gain + gn_bias).astype(jnp.bfloat16).reshape(FRAMES, H, W, C)
    padded = jnp.pad(activated, ((0, 0), (1, 1), (1, 1), (0, 0)))
    conv_sum = jnp.zeros((FRAMES * PIX, C), jnp.float32)
    for tap_index in range(9):
        row_shift, col_shift = divmod(tap_index, 3)
        window = padded[:, row_shift:row_shift + H, col_shift:col_shift + W, :].reshape(-1, C)
        conv_sum = conv_sum + jnp.dot(window, conv_weight[tap_index], preferred_element_type=jnp.float32)
    resid = joined.reshape(-1, C) + conv_sum
    token_mean = lax.optimization_barrier(jnp.mean(resid, axis=-1, keepdims=True))
    token_var = lax.optimization_barrier(jnp.mean(jnp.square(resid - token_mean), axis=-1, keepdims=True))
    normed = ((resid - token_mean) * lax.rsqrt(token_var + norm_epsilon) * ln_gain).astype(jnp.bfloat16)
    qkv_rows = jnp.dot(normed, qkv_weight, preferred_element_type=jnp.float32).astype(jnp.bfloat16)
    attended = attend_all(qkv_rows.reshape(FRAMES, PIX, 3 * C))
    output = resid + jnp.dot(attended.reshape(-1, C), out_weight, preferred_element_type=jnp.float32)
    return output.astype(jnp.bfloat16).reshape(FRAMES, PIX, C)
```

```python
import functools
import math

import jax
import jax.numpy as jnp
from jax import lax
from jax.experimental import pallas as pl
from jax.experimental.pallas import tpu as pltpu
from jax.sharding import PartitionSpec as P

HEADS = 10
HD = 64
GROUPS = 32
CLIP = 32
W = 32
LANES = 128

norm_epsilon = 1e-05
F32 = jnp.float32
BF16 = jnp.bfloat16
VMEM = pl.BlockSpec(memory_space=pltpu.VMEM)
SMEM = pl.BlockSpec(memory_space=pltpu.SMEM)


def params(mib):
    return pltpu.CompilerParams(vmem_limit_bytes=mib * 1024 * 1024)


def exact_dot(left, right, dims):
    return lax.dot_general(
        left, right, (dims, ((), ())), precision=lax.Precision.HIGHEST, preferred_element_type=F32
    )


def group_members(chans, first_lane):
    size = chans // GROUPS
    chan = lax.broadcasted_iota(jnp.int32, (chans, LANES), 0)
    start = (lax.broadcasted_iota(jnp.int32, (chans, LANES), 1) - first_lane) * size
    inside = (chan >= start) & (chan < start + size) & (start >= 0) & (start < chans)
    return inside.astype(F32)


def join_kernel(skip_ref, control_ref, weight_ref, joined_ref, stats_ref):
    pixels, chans = skip_ref.shape
    zero_out = jnp.dot(control_ref[...], weight_ref[...], preferred_element_type=F32).astype(BF16)
    joined = skip_ref[...].astype(F32) + zero_out.astype(F32)
    joined_ref[...] = joined
    sum_lanes = group_members(chans, 0)
    sq_lanes = group_members(chans, GROUPS)
    sums = jnp.broadcast_to(jnp.sum(joined, axis=0, keepdims=True), (8, chans))
    group_sums = exact_dot(sums, sum_lanes, ((1,), (0,)))
    group_mean = group_sums * (1.0 / (pixels * (chans // GROUPS)))
    chan_mean = exact_dot(group_mean, sum_lanes, ((1,), (1,)))[:1]
    spread = jnp.sum(jnp.square(joined - chan_mean), axis=0, keepdims=True)
    group_spread = exact_dot(jnp.broadcast_to(spread, (8, chans)), sq_lanes, ((1,), (0,)))
    stats_ref[...] = jnp.broadcast_to((group_sums + group_spread)[:1], stats_ref.shape)


def conv_kernel(
    clip_ref, joined_ref, stats_ref, gain_ref, bias_ref, weight_ref, resid_ref, window_ref
):
    pixels, chans = joined_ref.shape
    frames = stats_ref.shape[0]
    per_frame = float(pixels * (chans // GROUPS))
    stats = stats_ref[...]
    if frames > CLIP:
        row = lax.broadcasted_iota(jnp.int32, (frames, LANES), 0)
        first = clip_ref[0] * CLIP
        member = (row >= first) & (row < first + CLIP)
    else:
        member = jnp.full((frames, LANES), True)
    stats = jnp.where(member, stats, 0.0)
    mean_rows = stats * (1.0 / per_frame)
    lane_mean = jnp.sum(mean_rows, axis=0, keepdims=True) * (1.0 / CLIP)
    between = jnp.where(member, jnp.square(mean_rows - lane_mean), 0.0)
    lane_between = jnp.sum(between, axis=0, keepdims=True) * (1.0 / CLIP)
    lane_id = lax.broadcasted_iota(jnp.int32, (8, LANES), 1)
    lane_mean = jnp.broadcast_to(lane_mean, (8, LANES))
    lane_between = jnp.broadcast_to(lane_between, (8, LANES))
    sum_lanes = group_members(chans, 0)
    both_lanes = sum_lanes + group_members(chans, GROUPS)
    lane_var = jnp.where(lane_id < GROUPS, lane_between, lane_mean)
    chan_mean = exact_dot(lane_mean, sum_lanes, ((1,), (1,)))[:1]
    chan_var = exact_dot(lane_var, both_lanes, ((1,), (1,)))[:1]
    joined = joined_ref[...]
    scaled = (joined - chan_mean) * lax.rsqrt(chan_var + norm_epsilon)
    activated = jax.nn.silu(scaled * gain_ref[...] + bias_ref[...])
    col = lax.rem(lax.broadcasted_iota(jnp.int32, (pixels, chans), 0), W)
    left = jnp.where(col == 0, 0.0, pltpu.roll(activated, 1, 0))
    right = jnp.where(col == W - 1, 0.0, pltpu.roll(activated, pixels - 1, 0))
    edge = jnp.zeros((W, 3 * chans), BF16)
    window_ref[:W] = edge
    window_ref[W + pixels :] = edge
    window_ref[W : W + pixels, :chans] = left.astype(BF16)
    window_ref[W : W + pixels, chans : 2 * chans] = activated.astype(BF16)
    window_ref[W : W + pixels, 2 * chans :] = right.astype(BF16)
    total = joined
    for shift in range(3):
        total = total + jnp.dot(
            window_ref[shift * W : shift * W + pixels],
            weight_ref[shift],
            preferred_element_type=F32,
        )
    resid_ref[...] = total.astype(BF16)


def attend_kernel(per_dev, resid_ref, gain_ref, qkv_ref, out_ref, result_ref, rows_ref, mixed_ref):
    rows, chans = resid_ref.shape
    resid = resid_ref[...].astype(F32)
    mean = jnp.mean(resid, axis=-1, keepdims=True)
    centred = resid - mean
    var = jnp.mean(jnp.square(centred), axis=-1, keepdims=True)
    normed = (centred * lax.rsqrt(var + norm_epsilon) * gain_ref[...]).astype(BF16)
    rows_ref[...] = jnp.dot(normed, qkv_ref[...], preferred_element_type=F32).astype(BF16)
    row = lax.broadcasted_iota(jnp.int32, (rows, rows), 0)
    col = lax.broadcasted_iota(jnp.int32, (rows, rows), 1)
    paired = lax.rem(row, per_dev) == lax.rem(col, per_dev)
    if rows > per_dev * CLIP:
        paired = paired & (lax.div(row, per_dev * CLIP) == lax.div(col, per_dev * CLIP))
    heads_in = LANES // HD
    head_lane = lax.broadcasted_iota(jnp.int32, (rows, LANES), 1)
    for block in range(chans // LANES):
        start = block * LANES
        queries = rows_ref[:, start : start + LANES]
        keys = rows_ref[:, chans + start : chans + start + LANES]
        values = rows_ref[:, 2 * chans + start : 2 * chans + start + LANES]
        mixed = jnp.zeros((rows, LANES), F32)
        for inner in range(heads_in):
            own = (head_lane >= inner * HD) & (head_lane < (inner + 1) * HD)
            head_queries = jnp.where(own, queries, jnp.zeros_like(queries))
            head_values = jnp.where(own, values, jnp.zeros_like(values))
            scores = lax.dot_general(
                head_queries, keys, (((1,), (1,)), ((), ())), preferred_element_type=F32
            ) * (1.0 / math.sqrt(HD))
            scores = jnp.where(paired, scores, -1e30)
            expon = jnp.exp(scores - jnp.max(scores, axis=-1, keepdims=True))
            weights = (expon / jnp.sum(expon, axis=-1, keepdims=True)).astype(BF16)
            mixed = mixed + jnp.dot(weights, head_values, preferred_element_type=F32)
        mixed_ref[:, start : start + LANES] = mixed.astype(BF16)
    result = resid + jnp.dot(mixed_ref[...], out_ref[...], preferred_element_type=F32)
    result_ref[...] = result.astype(BF16)


def exchange(blocks):
    return lax.all_to_all(blocks, "frames", split_axis=0, concat_axis=0, tiled=True)


def body(
    skip, control, zero_weight, gn_gain, gn_bias, conv_weight, ln_gain, qkv_weight, out_weight
):
    f_dev, pixels, chans = skip.shape
    devices = lax.axis_size("frames")
    frame_count, per_dev, _ = control.shape
    rows = frame_count * per_dev
    own_control = exchange(control.reshape(rows, chans)).reshape(devices, f_dev, per_dev, chans)
    first_frame = lax.axis_index("frames") * f_dev if frame_count > CLIP else jnp.int32(0)
    joined, stats = [], []
    for f in range(f_dev):
        frame_joined, frame_stats = pl.pallas_call(
            join_kernel,
            out_shape=(
                jax.ShapeDtypeStruct((pixels, chans), F32),
                jax.ShapeDtypeStruct((devices, LANES), F32),
            ),
            in_specs=[VMEM] * 3,
            out_specs=(VMEM, VMEM),
            compiler_params=params(12),
            name="join",
        )(skip[f], own_control[:, f].reshape(pixels, chans), zero_weight)
        joined.append(frame_joined)
        stats.append(frame_stats)
    all_stats = exchange(jnp.stack(stats, axis=1).reshape(devices * f_dev, LANES))
    resid = []
    for f in range(f_dev):
        resid.append(
            pl.pallas_call(
                conv_kernel,
                out_shape=jax.ShapeDtypeStruct((pixels, chans), BF16),
                in_specs=[SMEM] + [VMEM] * 5,
                out_specs=VMEM,
                scratch_shapes=[pltpu.VMEM((pixels + 2 * W, 3 * chans), BF16)],
                compiler_params=params(24),
                name="conv",
            )(
                ((first_frame + f) // CLIP).reshape(1),
                joined[f],
                all_stats,
                gn_gain.reshape(1, chans),
                gn_bias.reshape(1, chans),
                conv_weight.reshape(3, 3 * chans, chans),
            )
        )
    by_pixel = jnp.stack(resid).reshape(f_dev, devices, per_dev, chans)
    by_pixel = exchange(by_pixel.transpose(1, 0, 2, 3).reshape(rows, chans))
    result = pl.pallas_call(
        functools.partial(attend_kernel, per_dev),
        out_shape=jax.ShapeDtypeStruct((rows, chans), BF16),
        in_specs=[VMEM] * 4,
        out_specs=VMEM,
        scratch_shapes=[pltpu.VMEM((rows, 3 * chans), BF16), pltpu.VMEM((rows, chans), BF16)],
        compiler_params=params(24),
        name="attend",
    )(by_pixel, ln_gain.reshape(1, chans), qkv_weight, out_weight)
    output = exchange(result).reshape(devices, f_dev, per_dev, chans)
    return output.transpose(1, 0, 2, 3).reshape(f_dev, pixels, chans)


def solution(mesh):
    in_specs = (
        P(("groups", "frames"), None, None),
        P("groups", "frames", None),
        P(),
        P(),
        P(),
        P(),
        P(),
        P(),
        P(),
    )
    out_specs = P(("groups", "frames"), None, None)
    return jax.shard_map(body, mesh=mesh, in_specs=in_specs, out_specs=out_specs, check_vma=False)
```

```python
import functools
import math

import jax
import jax.numpy as jnp
from jax import lax
from jax.experimental import pallas as pl
from jax.experimental.pallas import tpu as pltpu
from jax.sharding import PartitionSpec as P

HEADS = 10
HD = 64
GROUPS = 32
CLIP = 32
W = 32
LANES = 128

norm_epsilon = 1e-05
F32 = jnp.float32
BF16 = jnp.bfloat16
VMEM = pl.BlockSpec(memory_space=pltpu.VMEM)
SMEM = pl.BlockSpec(memory_space=pltpu.SMEM)


def params(mib):
    return pltpu.CompilerParams(vmem_limit_bytes=mib * 1024 * 1024)


def exact_dot(left, right, dims):
    return lax.dot_general(
        left, right, (dims, ((), ())), precision=lax.Precision.HIGHEST, preferred_element_type=F32
    )


def group_members(chans, first_lane):
    size = chans // GROUPS
    chan = lax.broadcasted_iota(jnp.int32, (chans, LANES), 0)
    start = (lax.broadcasted_iota(jnp.int32, (chans, LANES), 1) - first_lane) * size
    inside = (chan >= start) & (chan < start + size) & (start >= 0) & (start < chans)
    return inside.astype(F32)


def join_kernel(skip_ref, control_ref, weight_ref, joined_ref, stats_ref):
    pixels, chans = skip_ref.shape
    zero_out = jnp.dot(control_ref[...], weight_ref[...], preferred_element_type=F32).astype(BF16)
    joined = skip_ref[...].astype(F32) + zero_out.astype(F32)
    joined_ref[...] = joined
    sum_lanes = group_members(chans, 0)
    sq_lanes = group_members(chans, GROUPS)
    sums = jnp.broadcast_to(jnp.sum(joined, axis=0, keepdims=True), (8, chans))
    group_sums = exact_dot(sums, sum_lanes, ((1,), (0,)))
    group_mean = group_sums * (1.0 / (pixels * (chans // GROUPS)))
    chan_mean = exact_dot(group_mean, sum_lanes, ((1,), (1,)))[:1]
    spread = jnp.sum(jnp.square(joined - chan_mean), axis=0, keepdims=True)
    group_spread = exact_dot(jnp.broadcast_to(spread, (8, chans)), sq_lanes, ((1,), (0,)))
    stats_ref[...] = jnp.broadcast_to((group_sums + group_spread)[:1], stats_ref.shape)


def conv_kernel(
    clip_ref, joined_ref, stats_ref, gain_ref, bias_ref, weight_ref, resid_ref, window_ref
):
    pixels, chans = joined_ref.shape
    frames = stats_ref.shape[0]
    per_frame = float(pixels * (chans // GROUPS))
    stats = stats_ref[...]
    if frames > CLIP:
        row = lax.broadcasted_iota(jnp.int32, (frames, LANES), 0)
        first = clip_ref[0] * CLIP
        member = (row >= first) & (row < first + CLIP)
    else:
        member = jnp.full((frames, LANES), True)
    stats = jnp.where(member, stats, 0.0)
    mean_rows = stats * (1.0 / per_frame)
    lane_mean = jnp.sum(mean_rows, axis=0, keepdims=True) * (1.0 / CLIP)
    between = jnp.where(member, jnp.square(mean_rows - lane_mean), 0.0)
    lane_between = jnp.sum(between, axis=0, keepdims=True) * (1.0 / CLIP)
    lane_id = lax.broadcasted_iota(jnp.int32, (8, LANES), 1)
    lane_mean = jnp.broadcast_to(lane_mean, (8, LANES))
    lane_between = jnp.broadcast_to(lane_between, (8, LANES))
    sum_lanes = group_members(chans, 0)
    both_lanes = sum_lanes + group_members(chans, GROUPS)
    lane_var = jnp.where(lane_id < GROUPS, lane_between, lane_mean)
    chan_mean = exact_dot(lane_mean, sum_lanes, ((1,), (1,)))[:1]
    chan_var = exact_dot(lane_var, both_lanes, ((1,), (1,)))[:1]
    joined = joined_ref[...]
    scaled = (joined - chan_mean) * lax.rsqrt(chan_var + norm_epsilon)
    activated = jax.nn.silu(scaled * gain_ref[...].reshape(1, chans) + bias_ref[...].reshape(1, chans))
    col = lax.rem(lax.broadcasted_iota(jnp.int32, (pixels, chans), 0), W)
    left = jnp.where(col == 0, 0.0, pltpu.roll(activated, 1, 0))
    right = jnp.where(col == W - 1, 0.0, pltpu.roll(activated, pixels - 1, 0))
    edge = jnp.zeros((W, 3 * chans), BF16)
    window_ref[:W] = edge
    window_ref[W + pixels :] = edge
    window_ref[W : W + pixels, :chans] = left.astype(BF16)
    window_ref[W : W + pixels, chans : 2 * chans] = activated.astype(BF16)
    window_ref[W : W + pixels, 2 * chans :] = right.astype(BF16)
    total = joined
    for shift in range(3):
        total = total + jnp.dot(
            window_ref[shift * W : shift * W + pixels],
            weight_ref[shift],
            preferred_element_type=F32,
        )
    resid_ref[...] = total.astype(BF16)


def attend_kernel(per_dev, resid_ref, gain_ref, qkv_ref, out_ref, result_ref, rows_ref, mixed_ref):
    rows, chans = resid_ref.shape
    resid = resid_ref[...].astype(F32)
    mean = jnp.mean(resid, axis=-1, keepdims=True)
    centred = resid - mean
    var = jnp.mean(jnp.square(centred), axis=-1, keepdims=True)
    normed = (centred * lax.rsqrt(var + norm_epsilon) * gain_ref[...].reshape(1, chans)).astype(BF16)
    rows_ref[...] = jnp.dot(normed, qkv_ref[...], preferred_element_type=F32).astype(BF16)
    row = lax.broadcasted_iota(jnp.int32, (rows, rows), 0)
    col = lax.broadcasted_iota(jnp.int32, (rows, rows), 1)
    paired = lax.rem(row, per_dev) == lax.rem(col, per_dev)
    if rows > per_dev * CLIP:
        paired = paired & (lax.div(row, per_dev * CLIP) == lax.div(col, per_dev * CLIP))
    heads_in = LANES // HD
    head_lane = lax.broadcasted_iota(jnp.int32, (rows, LANES), 1)
    for block in range(chans // LANES):
        start = block * LANES
        queries = rows_ref[:, start : start + LANES]
        keys = rows_ref[:, chans + start : chans + start + LANES]
        values = rows_ref[:, 2 * chans + start : 2 * chans + start + LANES]
        mixed = jnp.zeros((rows, LANES), F32)
        for inner in range(heads_in):
            own = (head_lane >= inner * HD) & (head_lane < (inner + 1) * HD)
            head_queries = jnp.where(own, queries, jnp.zeros_like(queries))
            head_values = jnp.where(own, values, jnp.zeros_like(values))
            scores = lax.dot_general(
                head_queries, keys, (((1,), (1,)), ((), ())), preferred_element_type=F32
            ) * (1.0 / math.sqrt(HD))
            scores = jnp.where(paired, scores, -1e30)
            expon = jnp.exp(scores - jnp.max(scores, axis=-1, keepdims=True))
            weights = (expon / jnp.sum(expon, axis=-1, keepdims=True)).astype(BF16)
            mixed = mixed + jnp.dot(weights, head_values, preferred_element_type=F32)
        mixed_ref[:, start : start + LANES] = mixed.astype(BF16)
    result = resid + jnp.dot(mixed_ref[...], out_ref[...], preferred_element_type=F32)
    result_ref[...] = result.astype(BF16)


def fetch_kernel(*refs):
    count = len(refs) // 2
    for i in range(count):
        refs[count + i][...] = refs[i][...]


def fetch(*arrays):
    size = sum(a.size * a.dtype.itemsize for a in arrays)
    return pl.pallas_call(
        fetch_kernel,
        out_shape=tuple(jax.ShapeDtypeStruct(a.shape, a.dtype) for a in arrays),
        in_specs=[VMEM] * len(arrays),
        out_specs=(VMEM,) * len(arrays),
        compiler_params=params(1),
        cost_estimate=cost(0, 2 * size),
        name="fetch",
    )(*arrays)


def cost(flops, moved):
    return pl.CostEstimate(flops=int(flops), bytes_accessed=int(moved), transcendentals=0)


def exchange(blocks):
    return lax.all_to_all(blocks, "frames", split_axis=0, concat_axis=0, tiled=True)


def body(
    skip, control, zero_weight, gn_gain, gn_bias, conv_weight, ln_gain, qkv_weight, out_weight
):
    f_dev, pixels, chans = skip.shape
    devices = lax.axis_size("frames")
    frame_count, per_dev, _ = control.shape
    rows = frame_count * per_dev
    own_control = exchange(control.reshape(rows, chans)).reshape(devices, f_dev, per_dev, chans)
    skip, zero_weight = fetch(skip, zero_weight)
    first_frame = lax.axis_index("frames") * f_dev if frame_count > CLIP else jnp.int32(0)
    joined, stats = [], []
    for f in range(f_dev):
        frame_joined, frame_stats = pl.pallas_call(
            join_kernel,
            out_shape=(
                jax.ShapeDtypeStruct((pixels, chans), F32),
                jax.ShapeDtypeStruct((devices, LANES), F32),
            ),
            in_specs=[VMEM] * 3,
            out_specs=(VMEM, VMEM),
            compiler_params=params(8),
            cost_estimate=cost(2 * pixels * chans * chans, 32e6),
            name="join",
        )(skip[f], own_control[:, f].reshape(pixels, chans), zero_weight)
        joined.append(frame_joined)
        stats.append(frame_stats)
    all_stats = exchange(jnp.stack(stats, axis=1).reshape(devices * f_dev, LANES))
    resid = []
    for f in range(f_dev):
        resid.append(
            pl.pallas_call(
                conv_kernel,
                out_shape=jax.ShapeDtypeStruct((pixels, chans), BF16),
                in_specs=[SMEM] + [VMEM] * 5,
                out_specs=VMEM,
                scratch_shapes=[pltpu.VMEM((pixels + 2 * W, 3 * chans), BF16)],
                compiler_params=params(14),
                cost_estimate=cost(18 * pixels * chans * chans, 9e6),
                name="conv",
            )(
                ((first_frame + f) // CLIP).reshape(1),
                joined[f],
                all_stats,
                gn_gain,
                gn_bias,
                conv_weight.reshape(3, 3 * chans, chans),
            )
        )
    by_pixel = jnp.stack(resid).reshape(f_dev, devices, per_dev, chans)
    by_pixel = exchange(by_pixel.transpose(1, 0, 2, 3).reshape(rows, chans))
    result = pl.pallas_call(
        functools.partial(attend_kernel, per_dev),
        out_shape=jax.ShapeDtypeStruct((rows, chans), BF16),
        in_specs=[VMEM] * 4,
        out_specs=VMEM,
        scratch_shapes=[pltpu.VMEM((rows, 3 * chans), BF16), pltpu.VMEM((rows, chans), BF16)],
        compiler_params=params(14),
        cost_estimate=cost(8 * rows * chans * chans, 4e6),
        name="attend",
    )(by_pixel, ln_gain, qkv_weight, out_weight)
    output = exchange(result).reshape(devices, f_dev, per_dev, chans)
    return output.transpose(1, 0, 2, 3).reshape(f_dev, pixels, chans)


def solution(mesh):
    in_specs = (
        P(("groups", "frames"), None, None),
        P("groups", "frames", None),
        P(),
        P(),
        P(),
        P(),
        P(),
        P(),
        P(),
    )
    out_specs = P(("groups", "frames"), None, None)
    return jax.shard_map(body, mesh=mesh, in_specs=in_specs, out_specs=out_specs, check_vma=False)
```

```python
import functools
import math

import jax
import jax.numpy as jnp
from jax import lax
from jax.experimental import pallas as pl
from jax.experimental.pallas import tpu as pltpu
from jax.sharding import PartitionSpec as P

HEADS = 10
HD = 64
GROUPS = 32
CLIP = 32
W = 32
LANES = 128

norm_epsilon = 1e-05
F32 = jnp.float32
BF16 = jnp.bfloat16
VMEM = pl.BlockSpec(memory_space=pltpu.VMEM)
SMEM = pl.BlockSpec(memory_space=pltpu.SMEM)


def params(mib):
    return pltpu.CompilerParams(vmem_limit_bytes=mib * 1024 * 1024)


def exact_dot(left, right, dims):
    return lax.dot_general(
        left, right, (dims, ((), ())), precision=lax.Precision.HIGHEST, preferred_element_type=F32
    )


def group_members(chans, first_lane):
    size = chans // GROUPS
    chan = lax.broadcasted_iota(jnp.int32, (chans, LANES), 0)
    start = (lax.broadcasted_iota(jnp.int32, (chans, LANES), 1) - first_lane) * size
    inside = (chan >= start) & (chan < start + size) & (start >= 0) & (start < chans)
    return inside.astype(F32)


def join_kernel(skip_ref, control_ref, weight_ref, joined_ref, stats_ref):
    pixels, chans = skip_ref.shape
    zero_out = jnp.dot(control_ref[...], weight_ref[...], preferred_element_type=F32).astype(BF16)
    joined = skip_ref[...].astype(F32) + zero_out.astype(F32)
    joined_ref[...] = joined
    sum_lanes = group_members(chans, 0)
    sq_lanes = group_members(chans, GROUPS)
    sums = jnp.broadcast_to(jnp.sum(joined, axis=0, keepdims=True), (8, chans))
    group_sums = exact_dot(sums, sum_lanes, ((1,), (0,)))
    group_mean = group_sums * (1.0 / (pixels * (chans // GROUPS)))
    chan_mean = exact_dot(group_mean, sum_lanes, ((1,), (1,)))[:1]
    spread = jnp.sum(jnp.square(joined - chan_mean), axis=0, keepdims=True)
    group_spread = exact_dot(jnp.broadcast_to(spread, (8, chans)), sq_lanes, ((1,), (0,)))
    stats_ref[...] = jnp.broadcast_to((group_sums + group_spread)[:1], stats_ref.shape)


def conv_kernel(
    clip_ref, joined_ref, stats_ref, gains_ref, weight_hbm, resid_ref, sent_ref, window_ref,
    weight_ref, sems,
):
    copies = [
        pltpu.make_async_copy(weight_hbm.at[tap], weight_ref.at[tap], sems.at[tap])
        for tap in range(9)
    ]
    for copy in copies:
        copy.start()
    pixels, chans = joined_ref.shape
    frames = stats_ref.shape[0]
    per_frame = float(pixels * (chans // GROUPS))
    stats = stats_ref[...]
    if frames > CLIP:
        row = lax.broadcasted_iota(jnp.int32, (frames, LANES), 0)
        first = clip_ref[0] * CLIP
        member = (row >= first) & (row < first + CLIP)
    else:
        member = jnp.full((frames, LANES), True)
    stats = jnp.where(member, stats, 0.0)
    mean_rows = stats * (1.0 / per_frame)
    lane_mean = jnp.sum(mean_rows, axis=0, keepdims=True) * (1.0 / CLIP)
    between = jnp.where(member, jnp.square(mean_rows - lane_mean), 0.0)
    lane_between = jnp.sum(between, axis=0, keepdims=True) * (1.0 / CLIP)
    lane_id = lax.broadcasted_iota(jnp.int32, (8, LANES), 1)
    lane_mean = jnp.broadcast_to(lane_mean, (8, LANES))
    lane_between = jnp.broadcast_to(lane_between, (8, LANES))
    sum_lanes = group_members(chans, 0)
    both_lanes = sum_lanes + group_members(chans, GROUPS)
    lane_var = jnp.where(lane_id < GROUPS, lane_between, lane_mean)
    chan_mean = exact_dot(lane_mean, sum_lanes, ((1,), (1,)))[:1]
    chan_var = exact_dot(lane_var, both_lanes, ((1,), (1,)))[:1]
    joined = joined_ref[...]
    scaled = (joined - chan_mean) * lax.rsqrt(chan_var + norm_epsilon)
    activated = jax.nn.silu(scaled * gains_ref[:1] + gains_ref[1:2])
    col = lax.rem(lax.broadcasted_iota(jnp.int32, (pixels, chans), 0), W)
    left = jnp.where(col == 0, 0.0, pltpu.roll(activated, 1, 0))
    right = jnp.where(col == W - 1, 0.0, pltpu.roll(activated, pixels - 1, 0))
    edge = jnp.zeros((W, 3 * chans), BF16)
    window_ref[:W] = edge
    window_ref[W + pixels :] = edge
    window_ref[W : W + pixels, :chans] = left.astype(BF16)
    window_ref[W : W + pixels, chans : 2 * chans] = activated.astype(BF16)
    window_ref[W : W + pixels, 2 * chans :] = right.astype(BF16)
    total = joined
    for shift in range(3):
        for copy in copies[3 * shift : 3 * shift + 3]:
            copy.wait()
        total = total + jnp.dot(
            window_ref[shift * W : shift * W + pixels],
            weight_ref[3 * shift : 3 * shift + 3].reshape(3 * chans, chans),
            preferred_element_type=F32,
        )
    resid_ref[...] = total
    sent_ref[...] = total.astype(BF16)


def attend_kernel(per_dev, resid_ref, gains_ref, qkv_ref, out_ref, result_ref, rows_ref, mixed_ref):
    rows, chans = resid_ref.shape
    resid = resid_ref[...].astype(F32)
    mean = jnp.mean(resid, axis=-1, keepdims=True)
    centred = resid - mean
    var = jnp.mean(jnp.square(centred), axis=-1, keepdims=True)
    normed = (centred * lax.rsqrt(var + norm_epsilon) * gains_ref[2:3]).astype(BF16)
    rows_ref[...] = jnp.dot(normed, qkv_ref[...], preferred_element_type=F32).astype(BF16)
    row = lax.broadcasted_iota(jnp.int32, (rows, rows), 0)
    col = lax.broadcasted_iota(jnp.int32, (rows, rows), 1)
    paired = lax.rem(row, per_dev) == lax.rem(col, per_dev)
    if rows > per_dev * CLIP:
        paired = paired & (lax.div(row, per_dev * CLIP) == lax.div(col, per_dev * CLIP))
    heads_in = LANES // HD
    head_lane = lax.broadcasted_iota(jnp.int32, (rows, LANES), 1)
    for block in range(chans // LANES):
        start = block * LANES
        queries = rows_ref[:, start : start + LANES]
        keys = rows_ref[:, chans + start : chans + start + LANES]
        values = rows_ref[:, 2 * chans + start : 2 * chans + start + LANES]
        mixed = jnp.zeros((rows, LANES), F32)
        for inner in range(heads_in):
            own = (head_lane >= inner * HD) & (head_lane < (inner + 1) * HD)
            head_queries = jnp.where(own, queries, jnp.zeros_like(queries))
            head_values = jnp.where(own, values, jnp.zeros_like(values))
            scores = lax.dot_general(
                head_queries, keys, (((1,), (1,)), ((), ())), preferred_element_type=F32
            ) * (1.0 / math.sqrt(HD))
            scores = jnp.where(paired, scores, -1e30)
            expon = jnp.exp(scores - jnp.max(scores, axis=-1, keepdims=True))
            weights = (expon / jnp.sum(expon, axis=-1, keepdims=True)).astype(BF16)
            mixed = mixed + jnp.dot(weights, head_values, preferred_element_type=F32)
        mixed_ref[:, start : start + LANES] = mixed.astype(BF16)
    result = jnp.dot(mixed_ref[...], out_ref[...], preferred_element_type=F32)
    result_ref[...] = result.astype(BF16)


def fetch_kernel(*refs):
    count = len(refs) // 2
    for i in range(count):
        refs[count + i][...] = refs[i][...]


def fetch(*arrays):
    size = sum(a.size * a.dtype.itemsize for a in arrays)
    return pl.pallas_call(
        fetch_kernel,
        out_shape=tuple(jax.ShapeDtypeStruct(a.shape, a.dtype) for a in arrays),
        in_specs=[VMEM] * len(arrays),
        out_specs=(VMEM,) * len(arrays),
        compiler_params=params(1),
        cost_estimate=cost(0, 2 * size),
        name="fetch",
    )(*arrays)


def cost(flops, moved):
    return pl.CostEstimate(flops=int(flops), bytes_accessed=int(moved), transcendentals=0)


def exchange(blocks):
    return lax.all_to_all(blocks, "frames", split_axis=0, concat_axis=0, tiled=True)


def body(
    skip, control, zero_weight, gn_gain, gn_bias, conv_weight, ln_gain, qkv_weight, out_weight
):
    f_dev, pixels, chans = skip.shape
    devices = lax.axis_size("frames")
    frame_count, per_dev, _ = control.shape
    rows = frame_count * per_dev
    own_control = exchange(control.reshape(rows, chans)).reshape(devices, f_dev, per_dev, chans)
    skip, gains = fetch(skip, jnp.stack((gn_gain, gn_bias, ln_gain)))
    first_frame = lax.axis_index("frames") * f_dev if frame_count > CLIP else jnp.int32(0)
    joined, stats = [], []
    for f in range(f_dev):
        frame_joined, frame_stats = pl.pallas_call(
            join_kernel,
            out_shape=(
                jax.ShapeDtypeStruct((pixels, chans), F32),
                jax.ShapeDtypeStruct((devices, LANES), F32),
            ),
            in_specs=[VMEM] * 3,
            out_specs=(VMEM, VMEM),
            compiler_params=params(8),
            cost_estimate=cost(2 * pixels * chans * chans, 32e6),
            name="join",
        )(skip[f], own_control[:, f].reshape(pixels, chans), zero_weight)
        joined.append(frame_joined)
        stats.append(frame_stats)
    all_stats = exchange(jnp.stack(stats, axis=1).reshape(devices * f_dev, LANES))
    resid, sent = [], []
    for f in range(f_dev):
        frame_resid, frame_sent = pl.pallas_call(
            conv_kernel,
            out_shape=(
                jax.ShapeDtypeStruct((pixels, chans), F32),
                jax.ShapeDtypeStruct((pixels, chans), BF16),
            ),
            in_specs=[SMEM] + [VMEM] * 3 + [pl.BlockSpec(memory_space=pl.ANY)],
            out_specs=(VMEM, VMEM),
            scratch_shapes=[
                pltpu.VMEM((pixels + 2 * W, 3 * chans), BF16),
                pltpu.VMEM(conv_weight.shape, BF16),
                pltpu.SemaphoreType.DMA((9,)),
            ],
            compiler_params=params(50),
            cost_estimate=cost(18 * pixels * chans * chans, 9e6),
            name="conv",
        )(((first_frame + f) // CLIP).reshape(1), joined[f], all_stats, gains, conv_weight)
        resid.append(frame_resid)
        sent.append(frame_sent)
    by_pixel = jnp.stack(sent).reshape(f_dev, devices, per_dev, chans)
    by_pixel = exchange(by_pixel.transpose(1, 0, 2, 3).reshape(rows, chans))
    result = pl.pallas_call(
        functools.partial(attend_kernel, per_dev),
        out_shape=jax.ShapeDtypeStruct((rows, chans), BF16),
        in_specs=[VMEM] * 4,
        out_specs=VMEM,
        scratch_shapes=[pltpu.VMEM((rows, 3 * chans), BF16), pltpu.VMEM((rows, chans), BF16)],
        compiler_params=params(14),
        cost_estimate=cost(8 * rows * chans * chans, 4e6),
        name="attend",
    )(by_pixel, gains, qkv_weight, out_weight)
    mixed = exchange(result).reshape(devices, f_dev, per_dev, chans)
    mixed = mixed.transpose(1, 0, 2, 3).reshape(f_dev, pixels, chans)
    return (jnp.stack(resid) + mixed.astype(F32)).astype(BF16)


def solution(mesh):
    in_specs = (
        P(("groups", "frames"), None, None),
        P("groups", "frames", None),
        P(),
        P(),
        P(),
        P(),
        P(),
        P(),
        P(),
    )
    out_specs = P(("groups", "frames"), None, None)
    return jax.shard_map(body, mesh=mesh, in_specs=in_specs, out_specs=out_specs, check_vma=False)
```

```python
import functools
import math

import jax
import jax.numpy as jnp
from jax import lax
from jax.experimental import pallas as pl
from jax.experimental.pallas import tpu as pltpu
from jax.sharding import PartitionSpec as P

HEADS = 10
HD = 64
GROUPS = 32
CLIP = 32
W = 32
LANES = 128

norm_epsilon = 1e-05
F32 = jnp.float32
BF16 = jnp.bfloat16
VMEM = pl.BlockSpec(memory_space=pltpu.VMEM)
SMEM = pl.BlockSpec(memory_space=pltpu.SMEM)


def params(mib):
    return pltpu.CompilerParams(vmem_limit_bytes=mib * 1024 * 1024)


def member_dot(left, members):
    rows = left.shape[0]
    parts, rest = [], left
    for _ in range(3):
        part = rest.astype(BF16)
        parts.append(part.astype(F32))
        rest = rest - parts[-1]
    stacked = jnp.concatenate(parts).astype(BF16)
    product = jnp.dot(stacked, members, preferred_element_type=F32)
    return product[:rows] + product[rows : 2 * rows] + product[2 * rows :]


def group_members(chans, axis):
    size = chans // GROUPS
    first = lax.rem(lax.broadcasted_iota(jnp.int32, (LANES, LANES), 1 - axis), GROUPS) * size
    inner = lax.broadcasted_iota(jnp.int32, (LANES, LANES), axis) - first
    blocks = []
    for start in range(0, chans, LANES):
        place = inner + start
        blocks.append(jnp.where((place >= 0) & (place < size), 1.0, 0.0).astype(BF16))
    return jnp.concatenate(blocks, axis=axis)


def join_kernel(
    skip_ref, control_ref, weight_ref, conv_hbm, joined_ref, stats_ref, conv_ref, sem
):
    copy = pltpu.make_async_copy(conv_hbm.at[pl.ds(0, 3)], conv_ref, sem)
    copy.start()
    pixels, chans = skip_ref.shape
    zero_out = jnp.dot(control_ref[...], weight_ref[...], preferred_element_type=F32).astype(BF16)
    joined = skip_ref[...].astype(F32) + zero_out.astype(F32)
    joined_ref[...] = joined
    members = group_members(chans, 0)
    sums = jnp.broadcast_to(jnp.sum(joined, axis=0, keepdims=True), (8, chans))
    group_sums = member_dot(sums, members)
    lane_id = lax.broadcasted_iota(jnp.int32, (8, LANES), 1)
    group_mean = jnp.where(lane_id < GROUPS, group_sums, 0.0)
    group_mean = group_mean * (1.0 / (pixels * (chans // GROUPS)))
    chan_mean = member_dot(group_mean, group_members(chans, 1))[:1]
    spread = jnp.sum(jnp.square(joined_ref[...] - chan_mean), axis=0, keepdims=True)
    group_spread = member_dot(jnp.broadcast_to(spread, (8, chans)), members)
    stats = jnp.where(lane_id < GROUPS, group_sums, group_spread)
    stats = jnp.where(lane_id < 2 * GROUPS, stats, 0.0)
    stats_ref[...] = jnp.broadcast_to(stats[:1], stats_ref.shape)
    copy.wait()


def conv_kernel(
    clip_ref, joined_ref, stats_ref, gains_ref, early_ref, weight_hbm, resid_ref, sent_ref,
    window_ref, weight_ref, sems,
):
    copies = [
        pltpu.make_async_copy(weight_hbm.at[tap + 3], weight_ref.at[tap], sems.at[tap])
        for tap in range(6)
    ]
    for copy in copies:
        copy.start()
    pixels, chans = joined_ref.shape
    frames = stats_ref.shape[0]
    per_frame = float(pixels * (chans // GROUPS))
    stats = stats_ref[...]
    if frames > CLIP:
        row = lax.broadcasted_iota(jnp.int32, (frames, LANES), 0)
        first = clip_ref[0] * CLIP
        member = (row >= first) & (row < first + CLIP)
    else:
        member = jnp.full((frames, LANES), True)
    stats = jnp.where(member, stats, 0.0)
    mean_rows = stats * (1.0 / per_frame)
    lane_mean = jnp.sum(mean_rows, axis=0, keepdims=True) * (1.0 / CLIP)
    between = jnp.where(member, jnp.square(mean_rows - lane_mean), 0.0)
    lane_between = jnp.sum(between, axis=0, keepdims=True) * (1.0 / CLIP)
    lane_id = lax.broadcasted_iota(jnp.int32, (8, LANES), 1)
    row_id = lax.broadcasted_iota(jnp.int32, (8, LANES), 0)
    lane_var = jnp.where(lane_id < GROUPS, lane_between, lane_mean)
    lane_mean = jnp.where(lane_id < GROUPS, lane_mean, 0.0)
    chan_stats = member_dot(
        jnp.where(row_id == 0, lane_mean, lane_var), group_members(chans, 1)
    )
    chan_mean, chan_var = chan_stats[:1], chan_stats[1:2]
    edge = jnp.zeros((W, 3 * chans), BF16)
    window_ref[:W] = edge
    window_ref[W + pixels :] = edge
    factor = lax.rsqrt(chan_var + norm_epsilon)
    gain, bias = gains_ref[:1], gains_ref[1:2]
    col = lax.broadcasted_iota(jnp.int32, (W, chans), 0)

    @pl.loop(0, pixels // W)
    def _(line):
        here = pl.ds(pl.multiple_of(line * W, W), W)
        there = pl.ds(pl.multiple_of(line * W + W, W), W)
        activated = jax.nn.silu((joined_ref[here] - chan_mean) * factor * gain + bias)
        left = jnp.where(col == 0, 0.0, pltpu.roll(activated, 1, 0))
        right = jnp.where(col == W - 1, 0.0, pltpu.roll(activated, W - 1, 0))
        window_ref[there, :chans] = left.astype(BF16)
        window_ref[there, chans : 2 * chans] = activated.astype(BF16)
        window_ref[there, 2 * chans :] = right.astype(BF16)

    total = joined_ref[...]
    for shift in range(3):
        if shift == 0:
            weights = early_ref[...]
        else:
            taps = slice(3 * shift - 3, 3 * shift)
            for copy in copies[taps]:
                copy.wait()
            weights = weight_ref[taps]
        total = total + jnp.dot(
            window_ref[shift * W : shift * W + pixels],
            weights.reshape(3 * chans, chans),
            preferred_element_type=F32,
        )
    resid_ref[...] = total
    sent_ref[...] = total.astype(BF16)


def attend_kernel(per_dev, resid_ref, gains_ref, qkv_ref, out_ref, result_ref, rows_ref, mixed_ref):
    rows, chans = resid_ref.shape
    resid = resid_ref[...].astype(F32)
    mean = jnp.mean(resid, axis=-1, keepdims=True)
    centred = resid - mean
    var = jnp.mean(jnp.square(centred), axis=-1, keepdims=True)
    normed = (centred * lax.rsqrt(var + norm_epsilon) * gains_ref[2:3]).astype(BF16)
    rows_ref[...] = jnp.dot(normed, qkv_ref[...], preferred_element_type=F32).astype(BF16)
    scale = math.log2(math.e) / math.sqrt(HD)
    clip_rows = per_dev * CLIP
    period = max(per_dev, 8)
    pixel = lax.rem(lax.broadcasted_iota(jnp.int32, (1, period, clip_rows), 1), per_dev)
    other = lax.rem(lax.broadcasted_iota(jnp.int32, (1, period, clip_rows), 2), per_dev)
    paired = pixel == other
    low_lanes = lax.broadcasted_iota(jnp.int32, (clip_rows, LANES), 1) < HD
    one = jnp.ones((clip_rows, LANES), BF16)
    zero = jnp.zeros((clip_rows, LANES), BF16)
    for first_row in range(0, rows, clip_rows):
        clip = slice(first_row, first_row + clip_rows)

        for block in range(chans // LANES):
            lanes = [
                slice(block * LANES + part * chans, (block + 1) * LANES + part * chans)
                for part in range(3)
            ]
            queries, keys, values = [rows_ref[clip, part] for part in lanes]
            pair_queries = jnp.concatenate(
                [jnp.where(low_lanes, queries, zero), jnp.where(low_lanes, zero, queries)]
            )
            scores = lax.dot_general(
                pair_queries, keys, (((1,), (1,)), ((), ())), preferred_element_type=F32
            ).reshape(2 * clip_rows // period, period, clip_rows)
            scores = jnp.where(paired, scores, -1e30)
            top = jnp.max(scores, axis=-1, keepdims=True)
            expon = jnp.exp2((scores - top) * scale)
            expon = expon.reshape(2 * clip_rows, clip_rows).astype(BF16)
            low = jnp.dot(
                expon[:clip_rows], jnp.where(low_lanes, values, one), preferred_element_type=F32
            )
            high = jnp.dot(
                expon[clip_rows:], jnp.where(low_lanes, one, values), preferred_element_type=F32
            )
            total = pltpu.roll(jnp.where(low_lanes, high, low), HD, 1)
            mixed = jnp.where(low_lanes, low, high) / total
            mixed_ref[clip, lanes[0]] = mixed.astype(BF16)
    result = jnp.dot(mixed_ref[...], out_ref[...], preferred_element_type=F32)
    result_ref[...] = result.astype(BF16)


def fetch_kernel(*refs):
    count = len(refs) // 2
    for i in range(count):
        refs[count + i][...] = refs[i][...]


def fetch(*arrays):
    size = sum(a.size * a.dtype.itemsize for a in arrays)
    return pl.pallas_call(
        fetch_kernel,
        out_shape=tuple(jax.ShapeDtypeStruct(a.shape, a.dtype) for a in arrays),
        in_specs=[VMEM] * len(arrays),
        out_specs=(VMEM,) * len(arrays),
        compiler_params=params(1),
        cost_estimate=cost(0, 2 * size),
        name="fetch",
    )(*arrays)


def cost(flops, moved):
    return pl.CostEstimate(flops=int(flops), bytes_accessed=int(moved), transcendentals=0)


def exchange(blocks):
    return lax.all_to_all(blocks, "frames", split_axis=0, concat_axis=0, tiled=True)


def body(
    skip, control, zero_weight, gn_gain, gn_bias, conv_weight, ln_gain, qkv_weight, out_weight
):
    f_dev, pixels, chans = skip.shape
    devices = lax.axis_size("frames")
    frame_count, per_dev, _ = control.shape
    rows = frame_count * per_dev
    own_control = exchange(control.reshape(rows, chans)).reshape(devices, f_dev, per_dev, chans)
    gains = jnp.stack((gn_gain, gn_bias, ln_gain))
    skip, zero_weight, gains = fetch(skip, zero_weight, gains)
    first_frame = lax.axis_index("frames") * f_dev if frame_count > CLIP else jnp.int32(0)
    joined, stats, early = [], [], []
    for f in range(f_dev):
        frame_joined, frame_stats, frame_early = pl.pallas_call(
            join_kernel,
            out_shape=(
                jax.ShapeDtypeStruct((pixels, chans), F32),
                jax.ShapeDtypeStruct((devices, LANES), F32),
                jax.ShapeDtypeStruct((3, chans, chans), BF16),
            ),
            in_specs=[VMEM] * 3 + [pl.BlockSpec(memory_space=pl.ANY)],
            out_specs=(VMEM,) * 3,
            scratch_shapes=[pltpu.SemaphoreType.DMA],
            compiler_params=params(44),
            cost_estimate=cost(2 * pixels * chans * chans, 32e6),
            name="join",
        )(skip[f], own_control[:, f].reshape(pixels, chans), zero_weight, conv_weight)
        joined.append(frame_joined)
        stats.append(frame_stats)
        early.append(frame_early)
    all_stats = exchange(jnp.stack(stats, axis=1).reshape(devices * f_dev, LANES))
    resid, sent = [], []
    for f in range(f_dev):
        frame_resid, frame_sent = pl.pallas_call(
            conv_kernel,
            out_shape=(
                jax.ShapeDtypeStruct((pixels, chans), F32),
                jax.ShapeDtypeStruct((pixels, chans), BF16),
            ),
            in_specs=[SMEM] + [VMEM] * 4 + [pl.BlockSpec(memory_space=pl.ANY)],
            out_specs=(VMEM, VMEM),
            scratch_shapes=[
                pltpu.VMEM((pixels + 2 * W, 3 * chans), BF16),
                pltpu.VMEM((6, chans, chans), BF16),
                pltpu.SemaphoreType.DMA((6,)),
            ],
            compiler_params=params(50),
            cost_estimate=cost(18 * pixels * chans * chans, 9e6),
            name="conv",
        )(
            ((first_frame + f) // CLIP).reshape(1),
            joined[f],
            all_stats,
            gains,
            early[f],
            conv_weight,
        )
        resid.append(frame_resid)
        sent.append(frame_sent)
    by_pixel = jnp.stack(sent).reshape(f_dev, devices, per_dev, chans)
    by_pixel = exchange(by_pixel.transpose(1, 0, 2, 3).reshape(rows, chans))
    result = pl.pallas_call(
        functools.partial(attend_kernel, per_dev),
        out_shape=jax.ShapeDtypeStruct((rows, chans), BF16),
        in_specs=[VMEM] * 4,
        out_specs=VMEM,
        scratch_shapes=[pltpu.VMEM((rows, 3 * chans), BF16), pltpu.VMEM((rows, chans), BF16)],
        compiler_params=params(14),
        cost_estimate=cost(8 * rows * chans * chans, 4e6),
        name="attend",
    )(by_pixel, gains, qkv_weight, out_weight)
    mixed = exchange(result).reshape(devices, f_dev, per_dev, chans)
    mixed = mixed.transpose(1, 0, 2, 3).reshape(f_dev, pixels, chans)
    return (jnp.stack(resid) + mixed.astype(F32)).astype(BF16)


def solution(mesh):
    in_specs = (
        P(("groups", "frames"), None, None),
        P("groups", "frames", None),
        P(),
        P(),
        P(),
        P(),
        P(),
        P(),
        P(),
    )
    out_specs = P(("groups", "frames"), None, None)
    return jax.shard_map(body, mesh=mesh, in_specs=in_specs, out_specs=out_specs, check_vma=False)
```

```python
import functools
import math

import jax
import jax.numpy as jnp
from jax import lax
from jax.experimental import pallas as pl
from jax.experimental.pallas import tpu as pltpu
from jax.sharding import PartitionSpec as P

HEADS = 10
HD = 64
GROUPS = 32
CLIP = 32
W = 32
LANES = 128
EARLY = 2

norm_epsilon = 1e-05
F32 = jnp.float32
BF16 = jnp.bfloat16
VMEM = pl.BlockSpec(memory_space=pltpu.VMEM)
SMEM = pl.BlockSpec(memory_space=pltpu.SMEM)


def params(mib):
    return pltpu.CompilerParams(vmem_limit_bytes=mib * 1024 * 1024)


def member_dot(left, members):
    rows = left.shape[0]
    parts, rest = [], left
    for _ in range(3):
        part = rest.astype(BF16)
        parts.append(part.astype(F32))
        rest = rest - parts[-1]
    stacked = jnp.concatenate(parts).astype(BF16)
    product = jnp.dot(stacked, members, preferred_element_type=F32)
    return product[:rows] + product[rows : 2 * rows] + product[2 * rows :]


def group_members(chans, axis):
    size = chans // GROUPS
    first = lax.rem(lax.broadcasted_iota(jnp.int32, (LANES, LANES), 1 - axis), GROUPS) * size
    inner = lax.broadcasted_iota(jnp.int32, (LANES, LANES), axis) - first
    blocks = []
    for start in range(0, chans, LANES):
        place = inner + start
        blocks.append(jnp.where((place >= 0) & (place < size), 1.0, 0.0).astype(BF16))
    return jnp.concatenate(blocks, axis=axis)


def join_kernel(
    skip_ref, control_ref, weight_ref, conv_hbm, joined_ref, stats_ref, conv_ref, sem
):
    copy = pltpu.make_async_copy(conv_hbm.at[pl.ds(EARLY, 1)], conv_ref, sem)
    copy.start()
    pixels, chans = skip_ref.shape
    zero_out = jnp.dot(control_ref[...], weight_ref[...], preferred_element_type=F32).astype(BF16)
    joined = skip_ref[...].astype(F32) + zero_out.astype(F32)
    joined_ref[...] = joined
    members = group_members(chans, 0)
    sums = jnp.broadcast_to(jnp.sum(joined, axis=0, keepdims=True), (8, chans))
    group_sums = member_dot(sums, members)
    lane_id = lax.broadcasted_iota(jnp.int32, (8, LANES), 1)
    group_mean = jnp.where(lane_id < GROUPS, group_sums, 0.0)
    group_mean = group_mean * (1.0 / (pixels * (chans // GROUPS)))
    chan_mean = member_dot(group_mean, group_members(chans, 1))[:1]
    spread = jnp.sum(jnp.square(joined_ref[...] - chan_mean), axis=0, keepdims=True)
    group_spread = member_dot(jnp.broadcast_to(spread, (8, chans)), members)
    stats = jnp.where(lane_id < GROUPS, group_sums, group_spread)
    stats = jnp.where(lane_id < 2 * GROUPS, stats, 0.0)
    stats_ref[...] = jnp.broadcast_to(stats[:1], stats_ref.shape)
    copy.wait()


def conv_kernel(
    clip_ref, joined_ref, stats_ref, gains_ref, first_ref, early_ref, weight_hbm, resid_ref,
    sent_ref, window_ref, weight_ref, sems,
):
    copies = [
        pltpu.make_async_copy(weight_hbm.at[tap + 3], weight_ref.at[tap], sems.at[tap])
        for tap in range(6)
    ]
    for copy in copies:
        copy.start()
    pixels, chans = joined_ref.shape
    frames = stats_ref.shape[0]
    per_frame = float(pixels * (chans // GROUPS))
    stats = stats_ref[...]
    if frames > CLIP:
        row = lax.broadcasted_iota(jnp.int32, (frames, LANES), 0)
        first = clip_ref[0] * CLIP
        member = (row >= first) & (row < first + CLIP)
    else:
        member = jnp.full((frames, LANES), True)
    stats = jnp.where(member, stats, 0.0)
    mean_rows = stats * (1.0 / per_frame)
    lane_mean = jnp.sum(mean_rows, axis=0, keepdims=True) * (1.0 / CLIP)
    between = jnp.where(member, jnp.square(mean_rows - lane_mean), 0.0)
    lane_between = jnp.sum(between, axis=0, keepdims=True) * (1.0 / CLIP)
    lane_id = lax.broadcasted_iota(jnp.int32, (8, LANES), 1)
    row_id = lax.broadcasted_iota(jnp.int32, (8, LANES), 0)
    lane_var = jnp.where(lane_id < GROUPS, lane_between, lane_mean)
    lane_mean = jnp.where(lane_id < GROUPS, lane_mean, 0.0)
    chan_stats = member_dot(
        jnp.where(row_id == 0, lane_mean, lane_var), group_members(chans, 1)
    )
    chan_mean, chan_var = chan_stats[:1], chan_stats[1:2]
    edge = jnp.zeros((W, 3 * chans), BF16)
    window_ref[:W] = edge
    window_ref[W + pixels :] = edge
    factor = lax.rsqrt(chan_var + norm_epsilon)
    gain, bias = gains_ref[:1], gains_ref[1:2]
    col = lax.broadcasted_iota(jnp.int32, (W, chans), 0)

    @pl.loop(0, pixels // W)
    def _(line):
        here = pl.ds(pl.multiple_of(line * W, W), W)
        there = pl.ds(pl.multiple_of(line * W + W, W), W)
        activated = jax.nn.silu((joined_ref[here] - chan_mean) * factor * gain + bias)
        left = jnp.where(col == 0, 0.0, pltpu.roll(activated, 1, 0))
        right = jnp.where(col == W - 1, 0.0, pltpu.roll(activated, W - 1, 0))
        window_ref[there, :chans] = left.astype(BF16)
        window_ref[there, chans : 2 * chans] = activated.astype(BF16)
        window_ref[there, 2 * chans :] = right.astype(BF16)

    total = joined_ref[...]
    tap = 0
    for count in (EARLY, 1, 3, 3):
        if tap == 0:
            weights = first_ref[...]
        elif tap == EARLY:
            weights = early_ref[...]
        else:
            taps = slice(tap - 3, tap - 3 + count)
            for copy in copies[taps]:
                copy.wait()
            weights = weight_ref[taps]
        row = tap // 3 * W
        start = tap % 3 * chans
        total = total + jnp.dot(
            window_ref[row : row + pixels, start : start + count * chans],
            weights.reshape(count * chans, chans),
            preferred_element_type=F32,
        )
        tap += count
    resid_ref[...] = total
    sent_ref[...] = total.astype(BF16)


def attend_kernel(
    per_dev, resid_ref, gains_ref, qkv_ref, out_ref, result_ref, rows_ref, mixed_ref, scores_ref,
    weights_ref,
):
    rows, chans = resid_ref.shape
    resid = resid_ref[...].astype(F32)
    mean = jnp.mean(resid, axis=-1, keepdims=True)
    centred = resid - mean
    var = jnp.mean(jnp.square(centred), axis=-1, keepdims=True)
    normed = (centred * lax.rsqrt(var + norm_epsilon) * gains_ref[2:3]).astype(BF16)
    rows_ref[...] = jnp.dot(normed, qkv_ref[...], preferred_element_type=F32).astype(BF16)
    scale = math.log2(math.e) / math.sqrt(HD)
    clip_rows = per_dev * CLIP
    period = max(per_dev, 8)
    pixel = lax.rem(lax.broadcasted_iota(jnp.int32, (1, period, clip_rows), 1), per_dev)
    other = lax.rem(lax.broadcasted_iota(jnp.int32, (1, period, clip_rows), 2), per_dev)
    paired = pixel == other
    low_lanes = lax.broadcasted_iota(jnp.int32, (clip_rows, LANES), 1) < HD
    one = jnp.ones((clip_rows, LANES), BF16)
    zero = jnp.zeros((clip_rows, LANES), BF16)
    for first_row in range(0, rows, clip_rows):
        clip = slice(first_row, first_row + clip_rows)

        blocks = chans // LANES

        def lanes_of(block, part):
            start = block * LANES + part * chans
            return rows_ref[clip, start : start + LANES]

        def scores_of(block):
            queries = lanes_of(block, 0)
            pair_queries = jnp.concatenate(
                [jnp.where(low_lanes, queries, zero), jnp.where(low_lanes, zero, queries)]
            )
            scores_ref[block % 2] = lax.dot_general(
                pair_queries,
                lanes_of(block, 1),
                (((1,), (1,)), ((), ())),
                preferred_element_type=F32,
            )

        def weights_of(block):
            scores = scores_ref[block % 2].reshape(2 * clip_rows // period, period, clip_rows)
            scores = jnp.where(paired, scores, -1e30)
            top = jnp.max(scores, axis=-1, keepdims=True)
            expon = jnp.exp2((scores - top) * scale)
            weights_ref[block % 2] = expon.reshape(2 * clip_rows, clip_rows).astype(BF16)

        def mix(block):
            values = lanes_of(block, 2)
            weights = weights_ref[block % 2]
            low = jnp.dot(
                weights[:clip_rows], jnp.where(low_lanes, values, one), preferred_element_type=F32
            )
            high = jnp.dot(
                weights[clip_rows:], jnp.where(low_lanes, one, values), preferred_element_type=F32
            )
            total = pltpu.roll(jnp.where(low_lanes, high, low), HD, 1)
            mixed = jnp.where(low_lanes, low, high) / total
            mixed_ref[clip, block * LANES : (block + 1) * LANES] = mixed.astype(BF16)

        scores_of(0)
        for block in range(blocks):
            if block + 1 < blocks:
                scores_of(block + 1)
            weights_of(block)
            if block:
                mix(block - 1)
        mix(blocks - 1)
    result = jnp.dot(mixed_ref[...], out_ref[...], preferred_element_type=F32)
    result_ref[...] = result.astype(BF16)


def fetch_kernel(count, *refs):
    sem = refs[-1]
    taps_hbm, taps_ref = refs[count], refs[-2]
    copy = pltpu.make_async_copy(taps_hbm.at[pl.ds(0, EARLY)], taps_ref, sem)
    copy.start()
    for i in range(count):
        refs[count + 1 + i][...] = refs[i][...]
    copy.wait()


def fetch(conv_weight, *arrays):
    count = len(arrays)
    size = sum(a.size * a.dtype.itemsize for a in arrays)
    shapes = [jax.ShapeDtypeStruct(a.shape, a.dtype) for a in arrays]
    shapes.append(jax.ShapeDtypeStruct((EARLY,) + conv_weight.shape[1:], conv_weight.dtype))
    return pl.pallas_call(
        functools.partial(fetch_kernel, count),
        out_shape=tuple(shapes),
        in_specs=[VMEM] * count + [pl.BlockSpec(memory_space=pl.ANY)],
        out_specs=(VMEM,) * (count + 1),
        scratch_shapes=[pltpu.SemaphoreType.DMA],
        compiler_params=params(44),
        cost_estimate=cost(0, 2 * size),
        name="fetch",
    )(*arrays, conv_weight)


def cost(flops, moved):
    return pl.CostEstimate(flops=int(flops), bytes_accessed=int(moved), transcendentals=0)


def exchange(blocks):
    return lax.all_to_all(blocks, "frames", split_axis=0, concat_axis=0, tiled=True)


def body(
    skip, control, zero_weight, gn_gain, gn_bias, conv_weight, ln_gain, qkv_weight, out_weight
):
    f_dev, pixels, chans = skip.shape
    devices = lax.axis_size("frames")
    frame_count, per_dev, _ = control.shape
    rows = frame_count * per_dev
    own_control = exchange(control.reshape(rows, chans)).reshape(devices, f_dev, per_dev, chans)
    gains = jnp.stack((gn_gain, gn_bias, ln_gain))
    skip, zero_weight, gains, first_taps = fetch(conv_weight, skip, zero_weight, gains)
    first_frame = lax.axis_index("frames") * f_dev if frame_count > CLIP else jnp.int32(0)
    joined, stats, early = [], [], []
    for f in range(f_dev):
        frame_joined, frame_stats, frame_early = pl.pallas_call(
            join_kernel,
            out_shape=(
                jax.ShapeDtypeStruct((pixels, chans), F32),
                jax.ShapeDtypeStruct((devices, LANES), F32),
                jax.ShapeDtypeStruct((1, chans, chans), BF16),
            ),
            in_specs=[VMEM] * 3 + [pl.BlockSpec(memory_space=pl.ANY)],
            out_specs=(VMEM,) * 3,
            scratch_shapes=[pltpu.SemaphoreType.DMA],
            compiler_params=params(48),
            cost_estimate=cost(2 * pixels * chans * chans, 32e6),
            name="join",
        )(skip[f], own_control[:, f].reshape(pixels, chans), zero_weight, conv_weight)
        joined.append(frame_joined)
        stats.append(frame_stats)
        early.append(frame_early)
    all_stats = exchange(jnp.stack(stats, axis=1).reshape(devices * f_dev, LANES))
    resid, sent = [], []
    for f in range(f_dev):
        frame_resid, frame_sent = pl.pallas_call(
            conv_kernel,
            out_shape=(
                jax.ShapeDtypeStruct((pixels, chans), F32),
                jax.ShapeDtypeStruct((pixels, chans), BF16),
            ),
            in_specs=[SMEM] + [VMEM] * 5 + [pl.BlockSpec(memory_space=pl.ANY)],
            out_specs=(VMEM, VMEM),
            scratch_shapes=[
                pltpu.VMEM((pixels + 2 * W, 3 * chans), BF16),
                pltpu.VMEM((6, chans, chans), BF16),
                pltpu.SemaphoreType.DMA((6,)),
            ],
            compiler_params=params(50),
            cost_estimate=cost(18 * pixels * chans * chans, 9e6),
            name="conv",
        )(
            ((first_frame + f) // CLIP).reshape(1),
            joined[f],
            all_stats,
            gains,
            first_taps,
            early[f],
            conv_weight,
        )
        resid.append(frame_resid)
        sent.append(frame_sent)
    by_pixel = jnp.stack(sent).reshape(f_dev, devices, per_dev, chans)
    by_pixel = exchange(by_pixel.transpose(1, 0, 2, 3).reshape(rows, chans))
    result = pl.pallas_call(
        functools.partial(attend_kernel, per_dev),
        out_shape=jax.ShapeDtypeStruct((rows, chans), BF16),
        in_specs=[VMEM] * 4,
        out_specs=VMEM,
        scratch_shapes=[
            pltpu.VMEM((rows, 3 * chans), BF16),
            pltpu.VMEM((rows, chans), BF16),
            pltpu.VMEM((2, 2 * per_dev * CLIP, per_dev * CLIP), F32),
            pltpu.VMEM((2, 2 * per_dev * CLIP, per_dev * CLIP), BF16),
        ],
        compiler_params=params(14),
        cost_estimate=cost(8 * rows * chans * chans, 4e6),
        name="attend",
    )(by_pixel, gains, qkv_weight, out_weight)
    mixed = exchange(result).reshape(devices, f_dev, per_dev, chans)
    mixed = mixed.transpose(1, 0, 2, 3).reshape(f_dev, pixels, chans)
    return (jnp.stack(resid) + mixed.astype(F32)).astype(BF16)


def solution(mesh):
    in_specs = (
        P(("groups", "frames"), None, None),
        P("groups", "frames", None),
        P(),
        P(),
        P(),
        P(),
        P(),
        P(),
        P(),
    )
    out_specs = P(("groups", "frames"), None, None)
    return jax.shard_map(body, mesh=mesh, in_specs=in_specs, out_specs=out_specs, check_vma=False)
```

```python
import functools
import math

import jax
import jax.numpy as jnp
from jax import lax
from jax.experimental import pallas as pl
from jax.experimental.pallas import tpu as pltpu
from jax.sharding import PartitionSpec as P

HEADS = 10
HD = 64
GROUPS = 32
CLIP = 32
W = 32
LANES = 128
EARLY = 2
COUNTS = (2, 1, 3, 3)

norm_epsilon = 1e-05
F32 = jnp.float32
BF16 = jnp.bfloat16
VMEM = pl.BlockSpec(memory_space=pltpu.VMEM)
SMEM = pl.BlockSpec(memory_space=pltpu.SMEM)


def params(mib):
    return pltpu.CompilerParams(vmem_limit_bytes=mib * 1024 * 1024)


def member_dot(left, members):
    rows = left.shape[0]
    parts, rest = [], left
    for _ in range(3):
        part = rest.astype(BF16)
        parts.append(part.astype(F32))
        rest = rest - parts[-1]
    stacked = jnp.concatenate(parts).astype(BF16)
    product = jnp.dot(stacked, members, preferred_element_type=F32)
    return product[:rows] + product[rows : 2 * rows] + product[2 * rows :]


def group_members(chans, axis):
    size = chans // GROUPS
    first = lax.rem(lax.broadcasted_iota(jnp.int32, (LANES, LANES), 1 - axis), GROUPS) * size
    inner = lax.broadcasted_iota(jnp.int32, (LANES, LANES), axis) - first
    blocks = []
    for start in range(0, chans, LANES):
        place = inner + start
        blocks.append(jnp.where((place >= 0) & (place < size), 1.0, 0.0).astype(BF16))
    return jnp.concatenate(blocks, axis=axis)


def join_kernel(skip_ref, control_ref, weight_ref, joined_ref, stats_ref):
    pixels, chans = skip_ref.shape
    zero_out = jnp.dot(control_ref[...], weight_ref[...], preferred_element_type=F32).astype(BF16)
    joined = skip_ref[...].astype(F32) + zero_out.astype(F32)
    joined_ref[...] = joined
    members = group_members(chans, 0)
    sums = jnp.broadcast_to(jnp.sum(joined, axis=0, keepdims=True), (8, chans))
    group_sums = member_dot(sums, members)
    lane_id = lax.broadcasted_iota(jnp.int32, (8, LANES), 1)
    group_mean = jnp.where(lane_id < GROUPS, group_sums, 0.0)
    group_mean = group_mean * (1.0 / (pixels * (chans // GROUPS)))
    chan_mean = member_dot(group_mean, group_members(chans, 1))[:1]
    spread = jnp.sum(jnp.square(joined_ref[...] - chan_mean), axis=0, keepdims=True)
    group_spread = member_dot(jnp.broadcast_to(spread, (8, chans)), members)
    stats = jnp.where(lane_id < GROUPS, group_sums, group_spread)
    stats = jnp.where(lane_id < 2 * GROUPS, stats, 0.0)
    stats_ref[...] = jnp.broadcast_to(stats[:1], stats_ref.shape)


def conv_kernel(
    clip_ref, joined_ref, stats_ref, gains_ref, first_ref, weight_hbm, resid_ref, sent_ref,
    window_ref, weight_ref, sems,
):
    copies = [
        pltpu.make_async_copy(weight_hbm.at[tap + EARLY], weight_ref.at[tap], sems.at[tap])
        for tap in range(9 - EARLY)
    ]
    for copy in copies:
        copy.start()
    pixels, chans = joined_ref.shape
    frames = stats_ref.shape[0]
    per_frame = float(pixels * (chans // GROUPS))
    stats = stats_ref[...]
    if frames > CLIP:
        row = lax.broadcasted_iota(jnp.int32, (frames, LANES), 0)
        first = clip_ref[0] * CLIP
        member = (row >= first) & (row < first + CLIP)
    else:
        member = jnp.full((frames, LANES), True)
    stats = jnp.where(member, stats, 0.0)
    mean_rows = stats * (1.0 / per_frame)
    lane_mean = jnp.sum(mean_rows, axis=0, keepdims=True) * (1.0 / CLIP)
    between = jnp.where(member, jnp.square(mean_rows - lane_mean), 0.0)
    lane_between = jnp.sum(between, axis=0, keepdims=True) * (1.0 / CLIP)
    lane_id = lax.broadcasted_iota(jnp.int32, (8, LANES), 1)
    row_id = lax.broadcasted_iota(jnp.int32, (8, LANES), 0)
    lane_var = jnp.where(lane_id < GROUPS, lane_between, lane_mean)
    lane_mean = jnp.where(lane_id < GROUPS, lane_mean, 0.0)
    chan_stats = member_dot(
        jnp.where(row_id == 0, lane_mean, lane_var), group_members(chans, 1)
    )
    chan_mean, chan_var = chan_stats[:1], chan_stats[1:2]
    edge = jnp.zeros((W, 3 * chans), BF16)
    window_ref[:W] = edge
    window_ref[W + pixels :] = edge
    factor = lax.rsqrt(chan_var + norm_epsilon)
    gain, bias = gains_ref[:1], gains_ref[1:2]
    col = lax.broadcasted_iota(jnp.int32, (W, chans), 0)

    @pl.loop(0, pixels // W)
    def _(line):
        here = pl.ds(pl.multiple_of(line * W, W), W)
        there = pl.ds(pl.multiple_of(line * W + W, W), W)
        activated = jax.nn.silu((joined_ref[here] - chan_mean) * factor * gain + bias)
        left = jnp.where(col == 0, 0.0, pltpu.roll(activated, 1, 0))
        right = jnp.where(col == W - 1, 0.0, pltpu.roll(activated, W - 1, 0))
        window_ref[there, :chans] = left.astype(BF16)
        window_ref[there, chans : 2 * chans] = activated.astype(BF16)
        window_ref[there, 2 * chans :] = right.astype(BF16)

    total = joined_ref[...]
    tap = 0
    for count in COUNTS:
        if tap == 0:
            weights = first_ref[...]
        else:
            taps = slice(tap - EARLY, tap - EARLY + count)
            for copy in copies[taps]:
                copy.wait()
            weights = weight_ref[taps]
        row = tap // 3 * W
        start = tap % 3 * chans
        total = total + jnp.dot(
            window_ref[row : row + pixels, start : start + count * chans],
            weights.reshape(count * chans, chans),
            preferred_element_type=F32,
        )
        tap += count
    resid_ref[...] = total
    sent_ref[...] = total.astype(BF16)


def attend_kernel(
    per_dev, resid_ref, gains_ref, qkv_ref, out_ref, result_ref, rows_ref, mixed_ref, scores_ref,
    weights_ref,
):
    rows, chans = resid_ref.shape
    resid = resid_ref[...].astype(F32)
    mean = jnp.mean(resid, axis=-1, keepdims=True)
    centred = resid - mean
    var = jnp.mean(jnp.square(centred), axis=-1, keepdims=True)
    normed = (centred * lax.rsqrt(var + norm_epsilon) * gains_ref[2:3]).astype(BF16)
    rows_ref[...] = jnp.dot(normed, qkv_ref[...], preferred_element_type=F32).astype(BF16)
    scale = math.log2(math.e) / math.sqrt(HD)
    clip_rows = per_dev * CLIP
    period = max(per_dev, 8)
    pixel = lax.rem(lax.broadcasted_iota(jnp.int32, (1, period, clip_rows), 1), per_dev)
    other = lax.rem(lax.broadcasted_iota(jnp.int32, (1, period, clip_rows), 2), per_dev)
    paired = pixel == other
    low_lanes = lax.broadcasted_iota(jnp.int32, (clip_rows, LANES), 1) < HD
    one = jnp.ones((clip_rows, LANES), BF16)
    zero = jnp.zeros((clip_rows, LANES), BF16)
    for first_row in range(0, rows, clip_rows):
        clip = slice(first_row, first_row + clip_rows)

        blocks = chans // LANES

        def lanes_of(block, part):
            start = block * LANES + part * chans
            return rows_ref[clip, start : start + LANES]

        def scores_of(block):
            queries = lanes_of(block, 0)
            pair_queries = jnp.concatenate(
                [jnp.where(low_lanes, queries, zero), jnp.where(low_lanes, zero, queries)]
            )
            scores_ref[block % 2] = lax.dot_general(
                pair_queries,
                lanes_of(block, 1),
                (((1,), (1,)), ((), ())),
                preferred_element_type=F32,
            )

        def weights_of(block):
            scores = scores_ref[block % 2].reshape(2 * clip_rows // period, period, clip_rows)
            scores = jnp.where(paired, scores, -1e30)
            top = jnp.max(scores, axis=-1, keepdims=True)
            expon = jnp.exp2((scores - top) * scale)
            weights_ref[block % 2] = expon.reshape(2 * clip_rows, clip_rows).astype(BF16)

        def mix(block):
            values = lanes_of(block, 2)
            weights = weights_ref[block % 2]
            low = jnp.dot(
                weights[:clip_rows], jnp.where(low_lanes, values, one), preferred_element_type=F32
            )
            high = jnp.dot(
                weights[clip_rows:], jnp.where(low_lanes, one, values), preferred_element_type=F32
            )
            total = pltpu.roll(jnp.where(low_lanes, high, low), HD, 1)
            mixed = jnp.where(low_lanes, low, high) / total
            mixed_ref[clip, block * LANES : (block + 1) * LANES] = mixed.astype(BF16)

        scores_of(0)
        for block in range(blocks):
            if block + 1 < blocks:
                scores_of(block + 1)
            weights_of(block)
            if block:
                mix(block - 1)
        mix(blocks - 1)
    result = jnp.dot(mixed_ref[...], out_ref[...], preferred_element_type=F32)
    result_ref[...] = result.astype(BF16)


def fetch_kernel(count, *refs):
    sem = refs[-1]
    taps_hbm, taps_ref = refs[count], refs[-2]
    copy = pltpu.make_async_copy(taps_hbm.at[pl.ds(0, EARLY)], taps_ref, sem)
    copy.start()
    for i in range(count):
        refs[count + 1 + i][...] = refs[i][...]
    copy.wait()


def fetch(conv_weight, *arrays):
    count = len(arrays)
    size = sum(a.size * a.dtype.itemsize for a in arrays)
    shapes = [jax.ShapeDtypeStruct(a.shape, a.dtype) for a in arrays]
    shapes.append(jax.ShapeDtypeStruct((EARLY,) + conv_weight.shape[1:], conv_weight.dtype))
    return pl.pallas_call(
        functools.partial(fetch_kernel, count),
        out_shape=tuple(shapes),
        in_specs=[VMEM] * count + [pl.BlockSpec(memory_space=pl.ANY)],
        out_specs=(VMEM,) * (count + 1),
        scratch_shapes=[pltpu.SemaphoreType.DMA],
        compiler_params=params(44),
        cost_estimate=cost(0, 2 * size),
        name="fetch",
    )(*arrays, conv_weight)


def cost(flops, moved):
    return pl.CostEstimate(flops=int(flops), bytes_accessed=int(moved), transcendentals=0)


def exchange(blocks):
    return lax.all_to_all(blocks, "frames", split_axis=0, concat_axis=0, tiled=True)


def body(
    skip, control, zero_weight, gn_gain, gn_bias, conv_weight, ln_gain, qkv_weight, out_weight
):
    f_dev, pixels, chans = skip.shape
    devices = lax.axis_size("frames")
    frame_count, per_dev, _ = control.shape
    rows = frame_count * per_dev
    own_control = exchange(control.reshape(rows, chans)).reshape(devices, f_dev, per_dev, chans)
    gains = jnp.stack((gn_gain, gn_bias, ln_gain))
    skip, zero_weight, gains, first_taps = fetch(conv_weight, skip, zero_weight, gains)
    first_frame = lax.axis_index("frames") * f_dev if frame_count > CLIP else jnp.int32(0)
    joined, stats = [], []
    for f in range(f_dev):
        frame_joined, frame_stats = pl.pallas_call(
            join_kernel,
            out_shape=(
                jax.ShapeDtypeStruct((pixels, chans), F32),
                jax.ShapeDtypeStruct((devices, LANES), F32),
            ),
            in_specs=[VMEM] * 3,
            out_specs=(VMEM, VMEM),
            compiler_params=params(8),
            cost_estimate=cost(2 * pixels * chans * chans, 32e6),
            name="join",
        )(skip[f], own_control[:, f].reshape(pixels, chans), zero_weight)
        joined.append(frame_joined)
        stats.append(frame_stats)
    all_stats = exchange(jnp.stack(stats, axis=1).reshape(devices * f_dev, LANES))
    resid, sent = [], []
    for f in range(f_dev):
        frame_resid, frame_sent = pl.pallas_call(
            conv_kernel,
            out_shape=(
                jax.ShapeDtypeStruct((pixels, chans), F32),
                jax.ShapeDtypeStruct((pixels, chans), BF16),
            ),
            in_specs=[SMEM] + [VMEM] * 4 + [pl.BlockSpec(memory_space=pl.ANY)],
            out_specs=(VMEM, VMEM),
            scratch_shapes=[
                pltpu.VMEM((pixels + 2 * W, 3 * chans), BF16),
                pltpu.VMEM((9 - EARLY, chans, chans), BF16),
                pltpu.SemaphoreType.DMA((9 - EARLY,)),
            ],
            compiler_params=params(50),
            cost_estimate=cost(18 * pixels * chans * chans, 9e6),
            name="conv",
        )(
            ((first_frame + f) // CLIP).reshape(1),
            joined[f],
            all_stats,
            gains,
            first_taps,
            conv_weight,
        )
        resid.append(frame_resid)
        sent.append(frame_sent)
    by_pixel = jnp.stack(sent).reshape(f_dev, devices, per_dev, chans)
    by_pixel = exchange(by_pixel.transpose(1, 0, 2, 3).reshape(rows, chans))
    result = pl.pallas_call(
        functools.partial(attend_kernel, per_dev),
        out_shape=jax.ShapeDtypeStruct((rows, chans), BF16),
        in_specs=[VMEM] * 4,
        out_specs=VMEM,
        scratch_shapes=[
            pltpu.VMEM((rows, 3 * chans), BF16),
            pltpu.VMEM((rows, chans), BF16),
            pltpu.VMEM((2, 2 * per_dev * CLIP, per_dev * CLIP), F32),
            pltpu.VMEM((2, 2 * per_dev * CLIP, per_dev * CLIP), BF16),
        ],
        compiler_params=params(14),
        cost_estimate=cost(8 * rows * chans * chans, 4e6),
        name="attend",
    )(by_pixel, gains, qkv_weight, out_weight)
    mixed = exchange(result).reshape(devices, f_dev, per_dev, chans)
    mixed = mixed.transpose(1, 0, 2, 3).reshape(f_dev, pixels, chans)
    return (jnp.stack(resid) + mixed.astype(F32)).astype(BF16)


def solution(mesh):
    in_specs = (
        P(("groups", "frames"), None, None),
        P("groups", "frames", None),
        P(),
        P(),
        P(),
        P(),
        P(),
        P(),
        P(),
    )
    out_specs = P(("groups", "frames"), None, None)
    return jax.shard_map(body, mesh=mesh, in_specs=in_specs, out_specs=out_specs, check_vma=False)
```

```python
import functools
import math

import jax
import jax.numpy as jnp
from jax import lax
from jax.experimental import pallas as pl
from jax.experimental.pallas import tpu as pltpu
from jax.sharding import PartitionSpec as P

HEADS = 10
HD = 64
GROUPS = 32
CLIP = 32
W = 32
LANES = 128
EARLY = 3
COUNTS = (3, 3, 3)

norm_epsilon = 1e-05
F32 = jnp.float32
BF16 = jnp.bfloat16
VMEM = pl.BlockSpec(memory_space=pltpu.VMEM)
SMEM = pl.BlockSpec(memory_space=pltpu.SMEM)


def params(mib):
    return pltpu.CompilerParams(vmem_limit_bytes=mib * 1024 * 1024)


def member_dot(left, members):
    rows = left.shape[0]
    parts, rest = [], left
    for _ in range(3):
        part = rest.astype(BF16)
        parts.append(part.astype(F32))
        rest = rest - parts[-1]
    stacked = jnp.concatenate(parts).astype(BF16)
    product = jnp.dot(stacked, members, preferred_element_type=F32)
    return product[:rows] + product[rows : 2 * rows] + product[2 * rows :]


def group_members(chans, axis):
    size = chans // GROUPS
    first = lax.rem(lax.broadcasted_iota(jnp.int32, (LANES, LANES), 1 - axis), GROUPS) * size
    inner = lax.broadcasted_iota(jnp.int32, (LANES, LANES), axis) - first
    blocks = []
    for start in range(0, chans, LANES):
        place = inner + start
        blocks.append(jnp.where((place >= 0) & (place < size), 1.0, 0.0).astype(BF16))
    return jnp.concatenate(blocks, axis=axis)


def join_kernel(skip_ref, control_ref, weight_ref, joined_ref, stats_ref):
    pixels, chans = skip_ref.shape
    zero_out = jnp.dot(control_ref[...], weight_ref[...], preferred_element_type=F32).astype(BF16)
    joined = skip_ref[...].astype(F32) + zero_out.astype(F32)
    joined_ref[...] = joined
    members = group_members(chans, 0)
    sums = jnp.broadcast_to(jnp.sum(joined, axis=0, keepdims=True), (8, chans))
    group_sums = member_dot(sums, members)
    lane_id = lax.broadcasted_iota(jnp.int32, (8, LANES), 1)
    group_mean = jnp.where(lane_id < GROUPS, group_sums, 0.0)
    group_mean = group_mean * (1.0 / (pixels * (chans // GROUPS)))
    chan_mean = member_dot(group_mean, group_members(chans, 1))[:1]
    spread = jnp.sum(jnp.square(joined_ref[...] - chan_mean), axis=0, keepdims=True)
    group_spread = member_dot(jnp.broadcast_to(spread, (8, chans)), members)
    stats = jnp.where(lane_id < GROUPS, group_sums, group_spread)
    stats = jnp.where(lane_id < 2 * GROUPS, stats, 0.0)
    stats_ref[...] = jnp.broadcast_to(stats[:1], stats_ref.shape)


def conv_kernel(
    clip_ref, joined_ref, stats_ref, gains_ref, first_ref, weight_hbm, resid_ref, sent_ref,
    window_ref, weight_ref, sems,
):
    copies = [
        pltpu.make_async_copy(weight_hbm.at[tap + EARLY], weight_ref.at[tap], sems.at[tap])
        for tap in range(9 - EARLY)
    ]
    for copy in copies:
        copy.start()
    pixels, chans = joined_ref.shape
    frames = stats_ref.shape[0]
    per_frame = float(pixels * (chans // GROUPS))
    stats = stats_ref[...]
    if frames > CLIP:
        row = lax.broadcasted_iota(jnp.int32, (frames, LANES), 0)
        first = clip_ref[0] * CLIP
        member = (row >= first) & (row < first + CLIP)
    else:
        member = jnp.full((frames, LANES), True)
    stats = jnp.where(member, stats, 0.0)
    mean_rows = stats * (1.0 / per_frame)
    lane_mean = jnp.sum(mean_rows, axis=0, keepdims=True) * (1.0 / CLIP)
    between = jnp.where(member, jnp.square(mean_rows - lane_mean), 0.0)
    lane_between = jnp.sum(between, axis=0, keepdims=True) * (1.0 / CLIP)
    lane_id = lax.broadcasted_iota(jnp.int32, (8, LANES), 1)
    row_id = lax.broadcasted_iota(jnp.int32, (8, LANES), 0)
    lane_var = jnp.where(lane_id < GROUPS, lane_between, lane_mean)
    lane_mean = jnp.where(lane_id < GROUPS, lane_mean, 0.0)
    chan_stats = member_dot(
        jnp.where(row_id == 0, lane_mean, lane_var), group_members(chans, 1)
    )
    chan_mean, chan_var = chan_stats[:1], chan_stats[1:2]
    edge = jnp.zeros((W, 3 * chans), BF16)
    window_ref[:W] = edge
    window_ref[W + pixels :] = edge
    factor = lax.rsqrt(chan_var + norm_epsilon)
    gain, bias = gains_ref[:1], gains_ref[1:2]
    col = lax.broadcasted_iota(jnp.int32, (W, chans), 0)

    @pl.loop(0, pixels // W)
    def _(line):
        here = pl.ds(pl.multiple_of(line * W, W), W)
        there = pl.ds(pl.multiple_of(line * W + W, W), W)
        activated = jax.nn.silu((joined_ref[here] - chan_mean) * factor * gain + bias)
        left = jnp.where(col == 0, 0.0, pltpu.roll(activated, 1, 0))
        right = jnp.where(col == W - 1, 0.0, pltpu.roll(activated, W - 1, 0))
        window_ref[there, :chans] = left.astype(BF16)
        window_ref[there, chans : 2 * chans] = activated.astype(BF16)
        window_ref[there, 2 * chans :] = right.astype(BF16)

    total = joined_ref[...]
    tap = 0
    for count in COUNTS:
        if tap == 0:
            weights = first_ref[...]
        else:
            taps = slice(tap - EARLY, tap - EARLY + count)
            for copy in copies[taps]:
                copy.wait()
            weights = weight_ref[taps]
        row = tap // 3 * W
        start = tap % 3 * chans
        total = total + jnp.dot(
            window_ref[row : row + pixels, start : start + count * chans],
            weights.reshape(count * chans, chans),
            preferred_element_type=F32,
        )
        tap += count
    resid_ref[...] = total
    sent_ref[...] = total.astype(BF16)


def attend_kernel(
    per_dev, resid_ref, gains_ref, qkv_ref, out_ref, result_ref, rows_ref, mixed_ref, scores_ref,
    weights_ref,
):
    rows, chans = resid_ref.shape
    resid = resid_ref[...].astype(F32)
    mean = jnp.mean(resid, axis=-1, keepdims=True)
    centred = resid - mean
    var = jnp.mean(jnp.square(centred), axis=-1, keepdims=True)
    normed = (centred * lax.rsqrt(var + norm_epsilon) * gains_ref[2:3]).astype(BF16)
    rows_ref[...] = jnp.dot(normed, qkv_ref[...], preferred_element_type=F32).astype(BF16)
    scale = math.log2(math.e) / math.sqrt(HD)
    clip_rows = per_dev * CLIP
    period = max(per_dev, 8)
    pixel = lax.rem(lax.broadcasted_iota(jnp.int32, (1, period, clip_rows), 1), per_dev)
    other = lax.rem(lax.broadcasted_iota(jnp.int32, (1, period, clip_rows), 2), per_dev)
    paired = pixel == other
    low_lanes = lax.broadcasted_iota(jnp.int32, (clip_rows, LANES), 1) < HD
    one = jnp.ones((clip_rows, LANES), BF16)
    zero = jnp.zeros((clip_rows, LANES), BF16)
    for first_row in range(0, rows, clip_rows):
        clip = slice(first_row, first_row + clip_rows)

        blocks = chans // LANES

        def lanes_of(block, part):
            start = block * LANES + part * chans
            return rows_ref[clip, start : start + LANES]

        def scores_of(block):
            queries = lanes_of(block, 0)
            pair_queries = jnp.concatenate(
                [jnp.where(low_lanes, queries, zero), jnp.where(low_lanes, zero, queries)]
            )
            scores_ref[block % 2] = lax.dot_general(
                pair_queries,
                lanes_of(block, 1),
                (((1,), (1,)), ((), ())),
                preferred_element_type=F32,
            )

        def weights_of(block):
            scores = scores_ref[block % 2].reshape(2 * clip_rows // period, period, clip_rows)
            scores = jnp.where(paired, scores, -1e30)
            top = jnp.max(scores, axis=-1, keepdims=True)
            expon = jnp.exp2((scores - top) * scale)
            weights_ref[block % 2] = expon.reshape(2 * clip_rows, clip_rows).astype(BF16)

        def mix(block):
            values = lanes_of(block, 2)
            weights = weights_ref[block % 2]
            low = jnp.dot(
                weights[:clip_rows], jnp.where(low_lanes, values, one), preferred_element_type=F32
            )
            high = jnp.dot(
                weights[clip_rows:], jnp.where(low_lanes, one, values), preferred_element_type=F32
            )
            total = pltpu.roll(jnp.where(low_lanes, high, low), HD, 1)
            mixed = jnp.where(low_lanes, low, high) / total
            mixed_ref[clip, block * LANES : (block + 1) * LANES] = mixed.astype(BF16)

        scores_of(0)
        for block in range(blocks):
            if block + 1 < blocks:
                scores_of(block + 1)
            weights_of(block)
            if block:
                mix(block - 1)
        mix(blocks - 1)
    result = jnp.dot(mixed_ref[...], out_ref[...], preferred_element_type=F32)
    result_ref[...] = result.astype(BF16)


def fetch_kernel(count, *refs):
    for i in range(count):
        refs[count + i][...] = refs[i][...]


def fetch(*arrays):
    size = sum(a.size * a.dtype.itemsize for a in arrays)
    return pl.pallas_call(
        functools.partial(fetch_kernel, len(arrays)),
        out_shape=tuple(jax.ShapeDtypeStruct(a.shape, a.dtype) for a in arrays),
        in_specs=[VMEM] * len(arrays),
        out_specs=(VMEM,) * len(arrays),
        compiler_params=params(1),
        cost_estimate=cost(0, 2 * size),
        name="fetch",
    )(*arrays)


def taps_kernel(taps_hbm, after_ref, taps_ref, sem):
    copy = pltpu.make_async_copy(taps_hbm.at[pl.ds(0, EARLY)], taps_ref, sem)
    copy.start()
    copy.wait()


def fetch_taps(conv_weight, after):
    shape = (EARLY,) + conv_weight.shape[1:]
    return pl.pallas_call(
        taps_kernel,
        out_shape=jax.ShapeDtypeStruct(shape, conv_weight.dtype),
        in_specs=[pl.BlockSpec(memory_space=pl.ANY), VMEM],
        out_specs=VMEM,
        scratch_shapes=[pltpu.SemaphoreType.DMA],
        compiler_params=params(48),
        cost_estimate=cost(0, 6e6),
        name="taps",
    )(conv_weight, after)


def cost(flops, moved):
    return pl.CostEstimate(flops=int(flops), bytes_accessed=int(moved), transcendentals=0)


def exchange(blocks):
    return lax.all_to_all(blocks, "frames", split_axis=0, concat_axis=0, tiled=True)


def body(
    skip, control, zero_weight, gn_gain, gn_bias, conv_weight, ln_gain, qkv_weight, out_weight
):
    f_dev, pixels, chans = skip.shape
    devices = lax.axis_size("frames")
    frame_count, per_dev, _ = control.shape
    rows = frame_count * per_dev
    own_control = exchange(control.reshape(rows, chans)).reshape(devices, f_dev, per_dev, chans)
    gains = jnp.stack((gn_gain, gn_bias, ln_gain))
    skip, zero_weight, gains = fetch(skip, zero_weight, gains)
    first_frame = lax.axis_index("frames") * f_dev if frame_count > CLIP else jnp.int32(0)
    joined, stats = [], []
    for f in range(f_dev):
        frame_joined, frame_stats = pl.pallas_call(
            join_kernel,
            out_shape=(
                jax.ShapeDtypeStruct((pixels, chans), F32),
                jax.ShapeDtypeStruct((devices, LANES), F32),
            ),
            in_specs=[VMEM] * 3,
            out_specs=(VMEM, VMEM),
            compiler_params=params(8),
            cost_estimate=cost(2 * pixels * chans * chans, 32e6),
            name="join",
        )(skip[f], own_control[:, f].reshape(pixels, chans), zero_weight)
        joined.append(frame_joined)
        stats.append(frame_stats)
    first_taps = fetch_taps(conv_weight, stats[0])
    all_stats = exchange(jnp.stack(stats, axis=1).reshape(devices * f_dev, LANES))
    resid, sent = [], []
    for f in range(f_dev):
        frame_resid, frame_sent = pl.pallas_call(
            conv_kernel,
            out_shape=(
                jax.ShapeDtypeStruct((pixels, chans), F32),
                jax.ShapeDtypeStruct((pixels, chans), BF16),
            ),
            in_specs=[SMEM] + [VMEM] * 4 + [pl.BlockSpec(memory_space=pl.ANY)],
            out_specs=(VMEM, VMEM),
            scratch_shapes=[
                pltpu.VMEM((pixels + 2 * W, 3 * chans), BF16),
                pltpu.VMEM((9 - EARLY, chans, chans), BF16),
                pltpu.SemaphoreType.DMA((9 - EARLY,)),
            ],
            compiler_params=params(50),
            cost_estimate=cost(18 * pixels * chans * chans, 9e6),
            name="conv",
        )(
            ((first_frame + f) // CLIP).reshape(1),
            joined[f],
            all_stats,
            gains,
            first_taps,
            conv_weight,
        )
        resid.append(frame_resid)
        sent.append(frame_sent)
    by_pixel = jnp.stack(sent).reshape(f_dev, devices, per_dev, chans)
    by_pixel = exchange(by_pixel.transpose(1, 0, 2, 3).reshape(rows, chans))
    result = pl.pallas_call(
        functools.partial(attend_kernel, per_dev),
        out_shape=jax.ShapeDtypeStruct((rows, chans), BF16),
        in_specs=[VMEM] * 4,
        out_specs=VMEM,
        scratch_shapes=[
            pltpu.VMEM((rows, 3 * chans), BF16),
            pltpu.VMEM((rows, chans), BF16),
            pltpu.VMEM((2, 2 * per_dev * CLIP, per_dev * CLIP), F32),
            pltpu.VMEM((2, 2 * per_dev * CLIP, per_dev * CLIP), BF16),
        ],
        compiler_params=params(14),
        cost_estimate=cost(8 * rows * chans * chans, 4e6),
        name="attend",
    )(by_pixel, gains, qkv_weight, out_weight)
    mixed = exchange(result).reshape(devices, f_dev, per_dev, chans)
    mixed = mixed.transpose(1, 0, 2, 3).reshape(f_dev, pixels, chans)
    return (jnp.stack(resid) + mixed.astype(F32)).astype(BF16)


def solution(mesh):
    in_specs = (
        P(("groups", "frames"), None, None),
        P("groups", "frames", None),
        P(),
        P(),
        P(),
        P(),
        P(),
        P(),
        P(),
    )
    out_specs = P(("groups", "frames"), None, None)
    return jax.shard_map(body, mesh=mesh, in_specs=in_specs, out_specs=out_specs, check_vma=False)
```

```python
import functools
import math

import jax
import jax.numpy as jnp
from jax import lax
from jax.experimental import pallas as pl
from jax.experimental.pallas import tpu as pltpu
from jax.sharding import PartitionSpec as P

HEADS = 10
HD = 64
GROUPS = 32
CLIP = 32
W = 32
LANES = 128
EARLY_BYTES = 2 * 1024 * 1024

norm_epsilon = 1e-05
F32 = jnp.float32
BF16 = jnp.bfloat16
VMEM = pl.BlockSpec(memory_space=pltpu.VMEM)
SMEM = pl.BlockSpec(memory_space=pltpu.SMEM)


def params(mib):
    return pltpu.CompilerParams(vmem_limit_bytes=mib * 1024 * 1024)


def member_dot(left, members):
    rows = left.shape[0]
    parts, rest = [], left
    for _ in range(3):
        part = rest.astype(BF16)
        parts.append(part.astype(F32))
        rest = rest - parts[-1]
    stacked = jnp.concatenate(parts).astype(BF16)
    product = jnp.dot(stacked, members, preferred_element_type=F32)
    return product[:rows] + product[rows : 2 * rows] + product[2 * rows :]


def group_members(chans, axis):
    size = chans // GROUPS
    first = lax.rem(lax.broadcasted_iota(jnp.int32, (LANES, LANES), 1 - axis), GROUPS) * size
    inner = lax.broadcasted_iota(jnp.int32, (LANES, LANES), axis) - first
    blocks = []
    for start in range(0, chans, LANES):
        place = inner + start
        blocks.append(jnp.where((place >= 0) & (place < size), 1.0, 0.0).astype(BF16))
    return jnp.concatenate(blocks, axis=axis)


def join_kernel(skip_ref, control_ref, weight_ref, joined_ref, stats_ref):
    pixels, chans = skip_ref.shape
    zero_out = jnp.dot(control_ref[...], weight_ref[...], preferred_element_type=F32).astype(BF16)
    joined = skip_ref[...].astype(F32) + zero_out.astype(F32)
    joined_ref[...] = joined
    members = group_members(chans, 0)
    sums = jnp.broadcast_to(jnp.sum(joined, axis=0, keepdims=True), (8, chans))
    group_sums = member_dot(sums, members)
    lane_id = lax.broadcasted_iota(jnp.int32, (8, LANES), 1)
    group_mean = jnp.where(lane_id < GROUPS, group_sums, 0.0)
    group_mean = group_mean * (1.0 / (pixels * (chans // GROUPS)))
    chan_mean = member_dot(group_mean, group_members(chans, 1))[:1]
    spread = jnp.sum(jnp.square(joined_ref[...] - chan_mean), axis=0, keepdims=True)
    group_spread = member_dot(jnp.broadcast_to(spread, (8, chans)), members)
    stats = jnp.where(lane_id < GROUPS, group_sums, group_spread)
    stats = jnp.where(lane_id < 2 * GROUPS, stats, 0.0)
    stats_ref[...] = jnp.broadcast_to(stats[:1], stats_ref.shape)


def weight_chunks(chans):
    line = 3 * chans
    early = min(line, EARLY_BYTES // (2 * chans) // 256 * 256)
    return early, line - early, line, 2 * chans, chans


def conv_kernel(
    clip_ref, joined_ref, stats_ref, gains_ref, first_ref, weight_hbm, resid_ref, sent_ref,
    window_ref, weight_ref, sems,
):
    chunks = weight_chunks(joined_ref.shape[1])
    early = chunks[0]
    copies, row = [], early
    for at, size in enumerate(chunks[1:]):
        copies.append(
            pltpu.make_async_copy(
                weight_hbm.at[pl.ds(row, size)], weight_ref.at[pl.ds(row - early, size)], sems.at[at]
            )
        )
        row += size
    for copy in copies:
        copy.start()
    pixels, chans = joined_ref.shape
    frames = stats_ref.shape[0]
    per_frame = float(pixels * (chans // GROUPS))
    stats = stats_ref[...]
    if frames > CLIP:
        row = lax.broadcasted_iota(jnp.int32, (frames, LANES), 0)
        first = clip_ref[0] * CLIP
        member = (row >= first) & (row < first + CLIP)
    else:
        member = jnp.full((frames, LANES), True)
    stats = jnp.where(member, stats, 0.0)
    mean_rows = stats * (1.0 / per_frame)
    lane_mean = jnp.sum(mean_rows, axis=0, keepdims=True) * (1.0 / CLIP)
    between = jnp.where(member, jnp.square(mean_rows - lane_mean), 0.0)
    lane_between = jnp.sum(between, axis=0, keepdims=True) * (1.0 / CLIP)
    lane_id = lax.broadcasted_iota(jnp.int32, (8, LANES), 1)
    row_id = lax.broadcasted_iota(jnp.int32, (8, LANES), 0)
    lane_var = jnp.where(lane_id < GROUPS, lane_between, lane_mean)
    lane_mean = jnp.where(lane_id < GROUPS, lane_mean, 0.0)
    chan_stats = member_dot(
        jnp.where(row_id == 0, lane_mean, lane_var), group_members(chans, 1)
    )
    chan_mean, chan_var = chan_stats[:1], chan_stats[1:2]
    edge = jnp.zeros((W, 3 * chans), BF16)
    window_ref[:W] = edge
    window_ref[W + pixels :] = edge
    factor = lax.rsqrt(chan_var + norm_epsilon)
    gain, bias = gains_ref[:1], gains_ref[1:2]
    col = lax.broadcasted_iota(jnp.int32, (W, chans), 0)

    @pl.loop(0, pixels // W)
    def _(line):
        here = pl.ds(pl.multiple_of(line * W, W), W)
        there = pl.ds(pl.multiple_of(line * W + W, W), W)
        activated = jax.nn.silu((joined_ref[here] - chan_mean) * factor * gain + bias)
        left = jnp.where(col == 0, 0.0, pltpu.roll(activated, 1, 0))
        right = jnp.where(col == W - 1, 0.0, pltpu.roll(activated, W - 1, 0))
        window_ref[there, :chans] = left.astype(BF16)
        window_ref[there, chans : 2 * chans] = activated.astype(BF16)
        window_ref[there, 2 * chans :] = right.astype(BF16)

    total = joined_ref[...]
    row = 0
    for at, size in enumerate(chunks):
        if at == 0:
            weights = first_ref[...]
        else:
            copies[at - 1].wait()
            weights = weight_ref[row - early : row - early + size]
        line, start = divmod(row, 3 * chans)
        total = total + jnp.dot(
            window_ref[line * W : line * W + pixels, start : start + size],
            weights,
            preferred_element_type=F32,
        )
        row += size
    resid_ref[...] = total
    sent_ref[...] = total.astype(BF16)


def attend_kernel(
    per_dev, resid_ref, gains_ref, qkv_ref, out_ref, result_ref, rows_ref, mixed_ref, scores_ref,
    weights_ref,
):
    rows, chans = resid_ref.shape
    resid = resid_ref[...].astype(F32)
    mean = jnp.mean(resid, axis=-1, keepdims=True)
    centred = resid - mean
    var = jnp.mean(jnp.square(centred), axis=-1, keepdims=True)
    normed = (centred * lax.rsqrt(var + norm_epsilon) * gains_ref[2:3]).astype(BF16)
    rows_ref[...] = jnp.dot(normed, qkv_ref[...], preferred_element_type=F32).astype(BF16)
    scale = math.log2(math.e) / math.sqrt(HD)
    clip_rows = per_dev * CLIP
    period = max(per_dev, 8)
    pixel = lax.rem(lax.broadcasted_iota(jnp.int32, (1, period, clip_rows), 1), per_dev)
    other = lax.rem(lax.broadcasted_iota(jnp.int32, (1, period, clip_rows), 2), per_dev)
    paired = pixel == other
    low_lanes = lax.broadcasted_iota(jnp.int32, (clip_rows, LANES), 1) < HD
    one = jnp.ones((clip_rows, LANES), BF16)
    zero = jnp.zeros((clip_rows, LANES), BF16)
    for first_row in range(0, rows, clip_rows):
        clip = slice(first_row, first_row + clip_rows)

        blocks = chans // LANES

        def lanes_of(block, part):
            start = block * LANES + part * chans
            return rows_ref[clip, start : start + LANES]

        def scores_of(block):
            queries = lanes_of(block, 0)
            pair_queries = jnp.concatenate(
                [jnp.where(low_lanes, queries, zero), jnp.where(low_lanes, zero, queries)]
            )
            scores_ref[block % 2] = lax.dot_general(
                pair_queries,
                lanes_of(block, 1),
                (((1,), (1,)), ((), ())),
                preferred_element_type=F32,
            )

        def weights_of(block):
            scores = scores_ref[block % 2].reshape(2 * clip_rows // period, period, clip_rows)
            scores = jnp.where(paired, scores, -1e30)
            top = jnp.max(scores, axis=-1, keepdims=True)
            expon = jnp.exp2((scores - top) * scale)
            weights_ref[block % 2] = expon.reshape(2 * clip_rows, clip_rows).astype(BF16)

        def mix(block):
            values = lanes_of(block, 2)
            weights = weights_ref[block % 2]
            low = jnp.dot(
                weights[:clip_rows], jnp.where(low_lanes, values, one), preferred_element_type=F32
            )
            high = jnp.dot(
                weights[clip_rows:], jnp.where(low_lanes, one, values), preferred_element_type=F32
            )
            total = pltpu.roll(jnp.where(low_lanes, high, low), HD, 1)
            mixed = jnp.where(low_lanes, low, high) / total
            mixed_ref[clip, block * LANES : (block + 1) * LANES] = mixed.astype(BF16)

        scores_of(0)
        for block in range(blocks):
            if block + 1 < blocks:
                scores_of(block + 1)
            weights_of(block)
            if block:
                mix(block - 1)
        mix(blocks - 1)
    result = jnp.dot(mixed_ref[...], out_ref[...], preferred_element_type=F32)
    result_ref[...] = result.astype(BF16)


def fetch_kernel(count, *refs):
    sem = refs[-1]
    taps_hbm, taps_ref = refs[count], refs[-2]
    copy = pltpu.make_async_copy(taps_hbm.at[pl.ds(0, taps_ref.shape[0])], taps_ref, sem)
    copy.start()
    for i in range(count):
        refs[count + 1 + i][...] = refs[i][...]
    copy.wait()


def fetch(conv_weight, *arrays):
    count = len(arrays)
    size = sum(a.size * a.dtype.itemsize for a in arrays)
    shapes = [jax.ShapeDtypeStruct(a.shape, a.dtype) for a in arrays]
    chans = conv_weight.shape[1]
    shapes.append(jax.ShapeDtypeStruct((weight_chunks(chans)[0], chans), conv_weight.dtype))
    return pl.pallas_call(
        functools.partial(fetch_kernel, count),
        out_shape=tuple(shapes),
        in_specs=[VMEM] * count + [pl.BlockSpec(memory_space=pl.ANY)],
        out_specs=(VMEM,) * (count + 1),
        scratch_shapes=[pltpu.SemaphoreType.DMA],
        compiler_params=params(44),
        cost_estimate=cost(0, 2 * size),
        name="fetch",
    )(*arrays, conv_weight)


def cost(flops, moved):
    return pl.CostEstimate(flops=int(flops), bytes_accessed=int(moved), transcendentals=0)


def exchange(blocks):
    return lax.all_to_all(blocks, "frames", split_axis=0, concat_axis=0, tiled=True)


def body(
    skip, control, zero_weight, gn_gain, gn_bias, conv_weight, ln_gain, qkv_weight, out_weight
):
    f_dev, pixels, chans = skip.shape
    devices = lax.axis_size("frames")
    frame_count, per_dev, _ = control.shape
    rows = frame_count * per_dev
    own_control = exchange(control.reshape(rows, chans)).reshape(devices, f_dev, per_dev, chans)
    conv_weight = conv_weight.reshape(9 * chans, chans)
    gains = jnp.stack((gn_gain, gn_bias, ln_gain))
    skip, zero_weight, gains, first_taps = fetch(conv_weight, skip, zero_weight, gains)
    first_frame = lax.axis_index("frames") * f_dev if frame_count > CLIP else jnp.int32(0)
    joined, stats = [], []
    for f in range(f_dev):
        frame_joined, frame_stats = pl.pallas_call(
            join_kernel,
            out_shape=(
                jax.ShapeDtypeStruct((pixels, chans), F32),
                jax.ShapeDtypeStruct((devices, LANES), F32),
            ),
            in_specs=[VMEM] * 3,
            out_specs=(VMEM, VMEM),
            compiler_params=params(8),
            cost_estimate=cost(2 * pixels * chans * chans, 32e6),
            name="join",
        )(skip[f], own_control[:, f].reshape(pixels, chans), zero_weight)
        joined.append(frame_joined)
        stats.append(frame_stats)
    all_stats = exchange(jnp.stack(stats, axis=1).reshape(devices * f_dev, LANES))
    resid, sent = [], []
    for f in range(f_dev):
        frame_resid, frame_sent = pl.pallas_call(
            conv_kernel,
            out_shape=(
                jax.ShapeDtypeStruct((pixels, chans), F32),
                jax.ShapeDtypeStruct((pixels, chans), BF16),
            ),
            in_specs=[SMEM] + [VMEM] * 4 + [pl.BlockSpec(memory_space=pl.ANY)],
            out_specs=(VMEM, VMEM),
            scratch_shapes=[
                pltpu.VMEM((pixels + 2 * W, 3 * chans), BF16),
                pltpu.VMEM((9 * chans - weight_chunks(chans)[0], chans), BF16),
                pltpu.SemaphoreType.DMA((4,)),
            ],
            compiler_params=params(50),
            cost_estimate=cost(18 * pixels * chans * chans, 9e6),
            name="conv",
        )(
            ((first_frame + f) // CLIP).reshape(1),
            joined[f],
            all_stats,
            gains,
            first_taps,
            conv_weight,
        )
        resid.append(frame_resid)
        sent.append(frame_sent)
    by_pixel = jnp.stack(sent).reshape(f_dev, devices, per_dev, chans)
    by_pixel = exchange(by_pixel.transpose(1, 0, 2, 3).reshape(rows, chans))
    result = pl.pallas_call(
        functools.partial(attend_kernel, per_dev),
        out_shape=jax.ShapeDtypeStruct((rows, chans), BF16),
        in_specs=[VMEM] * 4,
        out_specs=VMEM,
        scratch_shapes=[
            pltpu.VMEM((rows, 3 * chans), BF16),
            pltpu.VMEM((rows, chans), BF16),
            pltpu.VMEM((2, 2 * per_dev * CLIP, per_dev * CLIP), F32),
            pltpu.VMEM((2, 2 * per_dev * CLIP, per_dev * CLIP), BF16),
        ],
        compiler_params=params(14),
        cost_estimate=cost(8 * rows * chans * chans, 4e6),
        name="attend",
    )(by_pixel, gains, qkv_weight, out_weight)
    mixed = exchange(result).reshape(devices, f_dev, per_dev, chans)
    mixed = mixed.transpose(1, 0, 2, 3).reshape(f_dev, pixels, chans)
    return (jnp.stack(resid) + mixed.astype(F32)).astype(BF16)


def solution(mesh):
    in_specs = (
        P(("groups", "frames"), None, None),
        P("groups", "frames", None),
        P(),
        P(),
        P(),
        P(),
        P(),
        P(),
        P(),
    )
    out_specs = P(("groups", "frames"), None, None)
    return jax.shard_map(body, mesh=mesh, in_specs=in_specs, out_specs=out_specs, check_vma=False)
```

```python
import functools
import math

import jax
import jax.numpy as jnp
from jax import lax
from jax.experimental import pallas as pl
from jax.experimental.pallas import tpu as pltpu
from jax.sharding import PartitionSpec as P

HEADS = 10
HD = 64
GROUPS = 32
CLIP = 32
W = 32
LANES = 128
EARLY = 2
COUNTS = (2, 1, 3, 3)

norm_epsilon = 1e-05
F32 = jnp.float32
BF16 = jnp.bfloat16
VMEM = pl.BlockSpec(memory_space=pltpu.VMEM)
SMEM = pl.BlockSpec(memory_space=pltpu.SMEM)


def params(mib):
    return pltpu.CompilerParams(vmem_limit_bytes=mib * 1024 * 1024)


def member_dot(left, members):
    rows = left.shape[0]
    parts, rest = [], left
    for _ in range(3):
        part = rest.astype(BF16)
        parts.append(part.astype(F32))
        rest = rest - parts[-1]
    stacked = jnp.concatenate(parts).astype(BF16)
    product = jnp.dot(stacked, members, preferred_element_type=F32)
    return product[:rows] + product[rows : 2 * rows] + product[2 * rows :]


def group_members(chans, axis):
    size = chans // GROUPS
    first = lax.rem(lax.broadcasted_iota(jnp.int32, (LANES, LANES), 1 - axis), GROUPS) * size
    inner = lax.broadcasted_iota(jnp.int32, (LANES, LANES), axis) - first
    blocks = []
    for start in range(0, chans, LANES):
        place = inner + start
        blocks.append(jnp.where((place >= 0) & (place < size), 1.0, 0.0).astype(BF16))
    return jnp.concatenate(blocks, axis=axis)


def join_kernel(
    skip_ref, control_ref, weight_ref, gather_ref, spread_ref, joined_ref, stats_ref
):
    pixels, chans = skip_ref.shape
    zero_out = jnp.dot(control_ref[...], weight_ref[...], preferred_element_type=F32).astype(BF16)
    joined = skip_ref[...].astype(F32) + zero_out.astype(F32)
    joined_ref[...] = joined
    members = gather_ref[...]
    sums = jnp.broadcast_to(jnp.sum(joined, axis=0, keepdims=True), (8, chans))
    group_sums = member_dot(sums, members)
    lane_id = lax.broadcasted_iota(jnp.int32, (8, LANES), 1)
    group_mean = jnp.where(lane_id < GROUPS, group_sums, 0.0)
    group_mean = group_mean * (1.0 / (pixels * (chans // GROUPS)))
    chan_mean = member_dot(group_mean, spread_ref[...])[:1]
    spread = jnp.sum(jnp.square(joined_ref[...] - chan_mean), axis=0, keepdims=True)
    group_spread = member_dot(jnp.broadcast_to(spread, (8, chans)), members)
    stats = jnp.where(lane_id < GROUPS, group_sums, group_spread)
    stats = jnp.where(lane_id < 2 * GROUPS, stats, 0.0)
    stats_ref[...] = jnp.broadcast_to(stats[:1], stats_ref.shape)


def conv_kernel(
    clip_ref, joined_ref, stats_ref, spread_ref, gains_ref, first_ref, weight_hbm, resid_ref,
    sent_ref, window_ref, weight_ref, sems,
):
    copies = [
        pltpu.make_async_copy(weight_hbm.at[tap + EARLY], weight_ref.at[tap], sems.at[tap])
        for tap in range(9 - EARLY)
    ]
    for copy in copies:
        copy.start()
    pixels, chans = joined_ref.shape
    frames = stats_ref.shape[0]
    per_frame = float(pixels * (chans // GROUPS))
    stats = stats_ref[...]
    if frames > CLIP:
        row = lax.broadcasted_iota(jnp.int32, (frames, LANES), 0)
        first = clip_ref[0] * CLIP
        member = (row >= first) & (row < first + CLIP)
    else:
        member = jnp.full((frames, LANES), True)
    stats = jnp.where(member, stats, 0.0)
    mean_rows = stats * (1.0 / per_frame)
    lane_mean = jnp.sum(mean_rows, axis=0, keepdims=True) * (1.0 / CLIP)
    between = jnp.where(member, jnp.square(mean_rows - lane_mean), 0.0)
    lane_between = jnp.sum(between, axis=0, keepdims=True) * (1.0 / CLIP)
    lane_id = lax.broadcasted_iota(jnp.int32, (8, LANES), 1)
    row_id = lax.broadcasted_iota(jnp.int32, (8, LANES), 0)
    lane_var = jnp.where(lane_id < GROUPS, lane_between, lane_mean)
    lane_mean = jnp.where(lane_id < GROUPS, lane_mean, 0.0)
    chan_stats = member_dot(
        jnp.where(row_id == 0, lane_mean, lane_var), spread_ref[...]
    )
    chan_mean, chan_var = chan_stats[:1], chan_stats[1:2]
    edge = jnp.zeros((W, 3 * chans), BF16)
    window_ref[:W] = edge
    window_ref[W + pixels :] = edge
    factor = lax.rsqrt(chan_var + norm_epsilon)
    gain, bias = gains_ref[:1], gains_ref[1:2]
    col = lax.broadcasted_iota(jnp.int32, (W, chans), 0)

    @pl.loop(0, pixels // W)
    def _(line):
        here = pl.ds(pl.multiple_of(line * W, W), W)
        there = pl.ds(pl.multiple_of(line * W + W, W), W)
        activated = jax.nn.silu((joined_ref[here] - chan_mean) * factor * gain + bias)
        left = jnp.where(col == 0, 0.0, pltpu.roll(activated, 1, 0))
        right = jnp.where(col == W - 1, 0.0, pltpu.roll(activated, W - 1, 0))
        window_ref[there, :chans] = left.astype(BF16)
        window_ref[there, chans : 2 * chans] = activated.astype(BF16)
        window_ref[there, 2 * chans :] = right.astype(BF16)

    total = joined_ref[...]
    tap = 0
    for count in COUNTS:
        if tap == 0:
            weights = first_ref[...]
        else:
            taps = slice(tap - EARLY, tap - EARLY + count)
            for copy in copies[taps]:
                copy.wait()
            weights = weight_ref[taps]
        row = tap // 3 * W
        start = tap % 3 * chans
        total = total + jnp.dot(
            window_ref[row : row + pixels, start : start + count * chans],
            weights.reshape(count * chans, chans),
            preferred_element_type=F32,
        )
        tap += count
    resid_ref[...] = total
    sent_ref[...] = total.astype(BF16)


def attend_kernel(
    per_dev, resid_ref, gains_ref, qkv_ref, out_ref, result_ref, rows_ref, mixed_ref, scores_ref,
    weights_ref,
):
    rows, chans = resid_ref.shape
    resid = resid_ref[...].astype(F32)
    mean = jnp.mean(resid, axis=-1, keepdims=True)
    centred = resid - mean
    var = jnp.mean(jnp.square(centred), axis=-1, keepdims=True)
    normed = (centred * lax.rsqrt(var + norm_epsilon) * gains_ref[2:3]).astype(BF16)
    rows_ref[...] = jnp.dot(normed, qkv_ref[...], preferred_element_type=F32).astype(BF16)
    scale = math.log2(math.e) / math.sqrt(HD)
    clip_rows = per_dev * CLIP
    period = max(per_dev, 8)
    pixel = lax.rem(lax.broadcasted_iota(jnp.int32, (1, period, clip_rows), 1), per_dev)
    other = lax.rem(lax.broadcasted_iota(jnp.int32, (1, period, clip_rows), 2), per_dev)
    paired = pixel == other
    low_lanes = lax.broadcasted_iota(jnp.int32, (clip_rows, LANES), 1) < HD
    one = jnp.ones((clip_rows, LANES), BF16)
    zero = jnp.zeros((clip_rows, LANES), BF16)
    for first_row in range(0, rows, clip_rows):
        clip = slice(first_row, first_row + clip_rows)

        blocks = chans // LANES

        def lanes_of(block, part):
            start = block * LANES + part * chans
            return rows_ref[clip, start : start + LANES]

        def scores_of(block):
            queries = lanes_of(block, 0)
            pair_queries = jnp.concatenate(
                [jnp.where(low_lanes, queries, zero), jnp.where(low_lanes, zero, queries)]
            )
            scores_ref[block % 2] = lax.dot_general(
                pair_queries,
                lanes_of(block, 1),
                (((1,), (1,)), ((), ())),
                preferred_element_type=F32,
            )

        def weights_of(block):
            scores = scores_ref[block % 2].reshape(2 * clip_rows // period, period, clip_rows)
            scores = jnp.where(paired, scores, -1e30)
            top = jnp.max(scores, axis=-1, keepdims=True)
            expon = jnp.exp2((scores - top) * scale)
            weights_ref[block % 2] = expon.reshape(2 * clip_rows, clip_rows).astype(BF16)

        def mix(block):
            values = lanes_of(block, 2)
            weights = weights_ref[block % 2]
            low = jnp.dot(
                weights[:clip_rows], jnp.where(low_lanes, values, one), preferred_element_type=F32
            )
            high = jnp.dot(
                weights[clip_rows:], jnp.where(low_lanes, one, values), preferred_element_type=F32
            )
            total = pltpu.roll(jnp.where(low_lanes, high, low), HD, 1)
            mixed = jnp.where(low_lanes, low, high) / total
            mixed_ref[clip, block * LANES : (block + 1) * LANES] = mixed.astype(BF16)

        scores_of(0)
        for block in range(blocks):
            if block + 1 < blocks:
                scores_of(block + 1)
            weights_of(block)
            if block:
                mix(block - 1)
        mix(blocks - 1)
    result = jnp.dot(mixed_ref[...], out_ref[...], preferred_element_type=F32)
    result_ref[...] = result.astype(BF16)


def fetch_kernel(count, *refs):
    taps_hbm = refs[count]
    taps_ref, gather_ref, spread_ref, sem = refs[-4:]
    copy = pltpu.make_async_copy(taps_hbm.at[pl.ds(0, EARLY)], taps_ref, sem)
    copy.start()
    for i in range(count):
        refs[count + 1 + i][...] = refs[i][...]
    gather_ref[...] = group_members(gather_ref.shape[0], 0)
    spread_ref[...] = group_members(spread_ref.shape[1], 1)
    copy.wait()


def fetch(conv_weight, *arrays):
    count = len(arrays)
    chans = conv_weight.shape[2]
    size = sum(a.size * a.dtype.itemsize for a in arrays)
    shapes = [jax.ShapeDtypeStruct(a.shape, a.dtype) for a in arrays]
    shapes.append(jax.ShapeDtypeStruct((EARLY,) + conv_weight.shape[1:], conv_weight.dtype))
    shapes.append(jax.ShapeDtypeStruct((chans, LANES), BF16))
    shapes.append(jax.ShapeDtypeStruct((LANES, chans), BF16))
    return pl.pallas_call(
        functools.partial(fetch_kernel, count),
        out_shape=tuple(shapes),
        in_specs=[VMEM] * count + [pl.BlockSpec(memory_space=pl.ANY)],
        out_specs=(VMEM,) * (count + 3),
        scratch_shapes=[pltpu.SemaphoreType.DMA],
        compiler_params=params(44),
        cost_estimate=cost(0, 2 * size),
        name="fetch",
    )(*arrays, conv_weight)


def cost(flops, moved):
    return pl.CostEstimate(flops=int(flops), bytes_accessed=int(moved), transcendentals=0)


def exchange(blocks):
    return lax.all_to_all(blocks, "frames", split_axis=0, concat_axis=0, tiled=True)


def body(
    skip, control, zero_weight, gn_gain, gn_bias, conv_weight, ln_gain, qkv_weight, out_weight
):
    f_dev, pixels, chans = skip.shape
    devices = lax.axis_size("frames")
    frame_count, per_dev, _ = control.shape
    rows = frame_count * per_dev
    own_control = exchange(control.reshape(rows, chans)).reshape(devices, f_dev, per_dev, chans)
    gains = jnp.stack((gn_gain, gn_bias, ln_gain))
    skip, zero_weight, gains, first_taps, gather, spread = fetch(
        conv_weight, skip, zero_weight, gains
    )
    first_frame = lax.axis_index("frames") * f_dev if frame_count > CLIP else jnp.int32(0)
    joined, stats = [], []
    for f in range(f_dev):
        frame_joined, frame_stats = pl.pallas_call(
            join_kernel,
            out_shape=(
                jax.ShapeDtypeStruct((pixels, chans), F32),
                jax.ShapeDtypeStruct((devices, LANES), F32),
            ),
            in_specs=[VMEM] * 5,
            out_specs=(VMEM, VMEM),
            compiler_params=params(8),
            cost_estimate=cost(2 * pixels * chans * chans, 32e6),
            name="join",
        )(skip[f], own_control[:, f].reshape(pixels, chans), zero_weight, gather, spread)
        joined.append(frame_joined)
        stats.append(frame_stats)
    all_stats = exchange(jnp.stack(stats, axis=1).reshape(devices * f_dev, LANES))
    resid, sent = [], []
    for f in range(f_dev):
        frame_resid, frame_sent = pl.pallas_call(
            conv_kernel,
            out_shape=(
                jax.ShapeDtypeStruct((pixels, chans), F32),
                jax.ShapeDtypeStruct((pixels, chans), BF16),
            ),
            in_specs=[SMEM] + [VMEM] * 5 + [pl.BlockSpec(memory_space=pl.ANY)],
            out_specs=(VMEM, VMEM),
            scratch_shapes=[
                pltpu.VMEM((pixels + 2 * W, 3 * chans), BF16),
                pltpu.VMEM((9 - EARLY, chans, chans), BF16),
                pltpu.SemaphoreType.DMA((9 - EARLY,)),
            ],
            compiler_params=params(50),
            cost_estimate=cost(18 * pixels * chans * chans, 9e6),
            name="conv",
        )(
            ((first_frame + f) // CLIP).reshape(1),
            joined[f],
            all_stats,
            spread,
            gains,
            first_taps,
            conv_weight,
        )
        resid.append(frame_resid)
        sent.append(frame_sent)
    by_pixel = jnp.stack(sent).reshape(f_dev, devices, per_dev, chans)
    by_pixel = exchange(by_pixel.transpose(1, 0, 2, 3).reshape(rows, chans))
    result = pl.pallas_call(
        functools.partial(attend_kernel, per_dev),
        out_shape=jax.ShapeDtypeStruct((rows, chans), BF16),
        in_specs=[VMEM] * 4,
        out_specs=VMEM,
        scratch_shapes=[
            pltpu.VMEM((rows, 3 * chans), BF16),
            pltpu.VMEM((rows, chans), BF16),
            pltpu.VMEM((2, 2 * per_dev * CLIP, per_dev * CLIP), F32),
            pltpu.VMEM((2, 2 * per_dev * CLIP, per_dev * CLIP), BF16),
        ],
        compiler_params=params(14),
        cost_estimate=cost(8 * rows * chans * chans, 4e6),
        name="attend",
    )(by_pixel, gains, qkv_weight, out_weight)
    mixed = exchange(result).reshape(devices, f_dev, per_dev, chans)
    mixed = mixed.transpose(1, 0, 2, 3).reshape(f_dev, pixels, chans)
    return (jnp.stack(resid) + mixed.astype(F32)).astype(BF16)


def solution(mesh):
    in_specs = (
        P(("groups", "frames"), None, None),
        P("groups", "frames", None),
        P(),
        P(),
        P(),
        P(),
        P(),
        P(),
        P(),
    )
    out_specs = P(("groups", "frames"), None, None)
    return jax.shard_map(body, mesh=mesh, in_specs=in_specs, out_specs=out_specs, check_vma=False)
```

```python
import functools
import math

import jax
import jax.numpy as jnp
from jax import lax
from jax.experimental import pallas as pl
from jax.experimental.pallas import tpu as pltpu
from jax.sharding import PartitionSpec as P

HEADS = 10
HD = 64
GROUPS = 32
CLIP = 32
W = 32
LANES = 128
EARLY = 2
COUNTS = (2, 1, 3, 3)

norm_epsilon = 1e-05
F32 = jnp.float32
BF16 = jnp.bfloat16
VMEM = pl.BlockSpec(memory_space=pltpu.VMEM)
SMEM = pl.BlockSpec(memory_space=pltpu.SMEM)


def params(mib):
    return pltpu.CompilerParams(
        vmem_limit_bytes=mib * 1024 * 1024
    )


def member_dot(left, members):
    rows = left.shape[0]
    parts, rest = [], left
    for _ in range(3):
        part = rest.astype(BF16)
        parts.append(part.astype(F32))
        rest = rest - parts[-1]
    stacked = jnp.concatenate(parts).astype(BF16)
    product = jnp.dot(stacked, members, preferred_element_type=F32)
    return product[:rows] + product[rows : 2 * rows] + product[2 * rows :]


def group_members(chans, axis):
    size = chans // GROUPS
    first = lax.rem(lax.broadcasted_iota(jnp.int32, (LANES, LANES), 1 - axis), GROUPS) * size
    inner = lax.broadcasted_iota(jnp.int32, (LANES, LANES), axis) - first
    blocks = []
    for start in range(0, chans, LANES):
        place = inner + start
        blocks.append(jnp.where((place >= 0) & (place < size), 1.0, 0.0).astype(BF16))
    return jnp.concatenate(blocks, axis=axis)


def join_kernel(
    skip_ref, control_ref, weight_ref, gather_ref, spread_ref, joined_ref, stats_ref
):
    pixels, chans = skip_ref.shape
    zero_out = jnp.dot(control_ref[...], weight_ref[...], preferred_element_type=F32).astype(BF16)
    joined = skip_ref[...].astype(F32) + zero_out.astype(F32)
    joined_ref[...] = joined
    members = gather_ref[...]
    sums = jnp.broadcast_to(jnp.sum(joined, axis=0, keepdims=True), (8, chans))
    group_sums = member_dot(sums, members)
    lane_id = lax.broadcasted_iota(jnp.int32, (8, LANES), 1)
    group_mean = jnp.where(lane_id < GROUPS, group_sums, 0.0)
    group_mean = group_mean * (1.0 / (pixels * (chans // GROUPS)))
    chan_mean = member_dot(group_mean, spread_ref[...])[:1]
    spread = jnp.sum(jnp.square(joined_ref[...] - chan_mean), axis=0, keepdims=True)
    group_spread = member_dot(jnp.broadcast_to(spread, (8, chans)), members)
    stats = jnp.where(lane_id < GROUPS, group_sums, group_spread)
    stats = jnp.where(lane_id < 2 * GROUPS, stats, 0.0)
    stats_ref[...] = jnp.broadcast_to(stats[:1], stats_ref.shape)


def conv_kernel(
    clip_ref, joined_ref, stats_ref, spread_ref, gains_ref, first_ref, weight_hbm, resid_ref,
    sent_ref, window_ref, weight_ref, sems,
):
    copies = [
        pltpu.make_async_copy(weight_hbm.at[tap + EARLY], weight_ref.at[tap], sems.at[tap])
        for tap in range(9 - EARLY)
    ]
    for copy in copies:
        copy.start()
    pixels, chans = joined_ref.shape
    frames = stats_ref.shape[0]
    per_frame = float(pixels * (chans // GROUPS))
    stats = stats_ref[...]
    if frames > CLIP:
        row = lax.broadcasted_iota(jnp.int32, (frames, LANES), 0)
        first = clip_ref[0] * CLIP
        member = (row >= first) & (row < first + CLIP)
    else:
        member = jnp.full((frames, LANES), True)
    stats = jnp.where(member, stats, 0.0)
    mean_rows = stats * (1.0 / per_frame)
    lane_mean = jnp.sum(mean_rows, axis=0, keepdims=True) * (1.0 / CLIP)
    between = jnp.where(member, jnp.square(mean_rows - lane_mean), 0.0)
    lane_between = jnp.sum(between, axis=0, keepdims=True) * (1.0 / CLIP)
    lane_id = lax.broadcasted_iota(jnp.int32, (8, LANES), 1)
    row_id = lax.broadcasted_iota(jnp.int32, (8, LANES), 0)
    lane_var = jnp.where(lane_id < GROUPS, lane_between, lane_mean)
    lane_mean = jnp.where(lane_id < GROUPS, lane_mean, 0.0)
    chan_stats = member_dot(
        jnp.where(row_id == 0, lane_mean, lane_var), spread_ref[...]
    )
    chan_mean, chan_var = chan_stats[:1], chan_stats[1:2]
    edge = jnp.zeros((W, 3 * chans), BF16)
    window_ref[:W] = edge
    window_ref[W + pixels :] = edge
    factor = lax.rsqrt(chan_var + norm_epsilon)
    gain, bias = gains_ref[:1], gains_ref[1:2]
    col = lax.broadcasted_iota(jnp.int32, (W, chans), 0)

    @pl.loop(0, pixels // W)
    def _(line):
        here = pl.ds(pl.multiple_of(line * W, W), W)
        there = pl.ds(pl.multiple_of(line * W + W, W), W)
        activated = jax.nn.silu((joined_ref[here] - chan_mean) * factor * gain + bias)
        left = jnp.where(col == 0, 0.0, pltpu.roll(activated, 1, 0))
        right = jnp.where(col == W - 1, 0.0, pltpu.roll(activated, W - 1, 0))
        window_ref[there, :chans] = left.astype(BF16)
        window_ref[there, chans : 2 * chans] = activated.astype(BF16)
        window_ref[there, 2 * chans :] = right.astype(BF16)

    total = joined_ref[...]
    tap = 0
    for count in COUNTS:
        if tap == 0:
            weights = first_ref[...]
        else:
            taps = slice(tap - EARLY, tap - EARLY + count)
            for copy in copies[taps]:
                copy.wait()
            weights = weight_ref[taps]
        row = tap // 3 * W
        start = tap % 3 * chans
        total = total + jnp.dot(
            window_ref[row : row + pixels, start : start + count * chans],
            weights.reshape(count * chans, chans),
            preferred_element_type=F32,
        )
        tap += count
    resid_ref[...] = total
    sent_ref[...] = total.astype(BF16)


def moved_rows(rows, per_dev, groups):
    size = per_dev // groups
    old = lax.broadcasted_iota(jnp.int32, (1, rows), 1)
    frame, pixel = lax.div(old, per_dev), lax.rem(old, per_dev)
    part = lax.div(frame, CLIP) * groups + lax.div(pixel, size)
    return (part * CLIP + lax.rem(frame, CLIP)) * size + lax.rem(pixel, size)


def source_rows(rows, per_dev, groups):
    size = per_dev // groups
    new = lax.broadcasted_iota(jnp.int32, (1, rows), 1)
    part = lax.div(new, CLIP * size)
    frame = lax.div(part, groups) * CLIP + lax.rem(lax.div(new, size), CLIP)
    return frame * per_dev + lax.rem(part, groups) * size + lax.rem(new, size)


def select_rows(places, values):
    rows = values.shape[0]
    row = lax.broadcasted_iota(jnp.int32, (rows, rows), 0)
    return jnp.dot(
        jnp.where(row == places, 1.0, 0.0).astype(BF16), values, preferred_element_type=F32
    )


def attend_kernel(
    per_dev, resid_ref, gains_ref, qkv_ref, out_ref, result_ref, rows_ref, mixed_ref
):
    rows, chans = resid_ref.shape
    groups = max(1, per_dev * CLIP // LANES)
    size = per_dev // groups
    resid = resid_ref[...]
    if groups > 1:
        resid = select_rows(moved_rows(rows, per_dev, groups), resid)
    else:
        resid = resid.astype(F32)
    mean = jnp.mean(resid, axis=-1, keepdims=True)
    centred = resid - mean
    var = jnp.mean(jnp.square(centred), axis=-1, keepdims=True)
    normed = (centred * lax.rsqrt(var + norm_epsilon) * gains_ref[2:3]).astype(BF16)
    rows_ref[...] = jnp.dot(normed, qkv_ref[...], preferred_element_type=F32).astype(BF16)
    scale = math.log2(math.e) / math.sqrt(HD)
    part_rows = size * CLIP
    period = max(size, 8)
    pixel = lax.rem(lax.broadcasted_iota(jnp.int32, (1, period, part_rows), 1), size)
    other = lax.rem(lax.broadcasted_iota(jnp.int32, (1, period, part_rows), 2), size)
    paired = pixel == other
    low_lanes = lax.broadcasted_iota(jnp.int32, (part_rows, LANES), 1) < HD
    one = jnp.ones((part_rows, LANES), BF16)
    zero = jnp.zeros((part_rows, LANES), BF16)

    def lanes_of(part, block, which):
        start = block * LANES + which * chans
        return rows_ref[part * part_rows : (part + 1) * part_rows, start : start + LANES]

    def scores_of(part, block):
        queries = lanes_of(part, block, 0)
        pair_queries = jnp.concatenate(
            [jnp.where(low_lanes, queries, zero), jnp.where(low_lanes, zero, queries)]
        )
        return lax.dot_general(
            pair_queries,
            lanes_of(part, block, 1),
            (((1,), (1,)), ((), ())),
            preferred_element_type=F32,
        )

    def weights_of(scores):
        scores = scores.reshape(2 * part_rows // period, period, part_rows)
        scores = jnp.where(paired, scores, -1e30)
        top = jnp.max(scores, axis=-1, keepdims=True)
        expon = jnp.exp2((scores - top) * scale)
        return expon.reshape(2 * part_rows, part_rows).astype(BF16)

    def mix(part, block, weights):
        values = lanes_of(part, block, 2)
        low = jnp.dot(
            weights[:part_rows], jnp.where(low_lanes, values, one), preferred_element_type=F32
        )
        high = jnp.dot(
            weights[part_rows:], jnp.where(low_lanes, one, values), preferred_element_type=F32
        )
        total = pltpu.roll(jnp.where(low_lanes, high, low), HD, 1)
        mixed = jnp.where(low_lanes, low, high) / total
        mixed_ref[
            part * part_rows : (part + 1) * part_rows, block * LANES : (block + 1) * LANES
        ] = mixed.astype(BF16)

    units = [
        (part, block) for part in range(rows // part_rows) for block in range(chans // LANES)
    ]
    for unit in units:
        mix(*unit, weights_of(scores_of(*unit)))
    mixed = mixed_ref[...]
    if groups > 1:
        mixed = select_rows(source_rows(rows, per_dev, groups), mixed).astype(BF16)
    result = jnp.dot(mixed, out_ref[...], preferred_element_type=F32)
    result_ref[...] = result.astype(BF16)


def fetch_kernel(count, *refs):
    taps_hbm = refs[count]
    taps_ref, gather_ref, spread_ref, sem = refs[-4:]
    copy = pltpu.make_async_copy(taps_hbm.at[pl.ds(0, EARLY)], taps_ref, sem)
    copy.start()
    for i in range(count):
        refs[count + 1 + i][...] = refs[i][...]
    gather_ref[...] = group_members(gather_ref.shape[0], 0)
    spread_ref[...] = group_members(spread_ref.shape[1], 1)
    copy.wait()


def fetch(conv_weight, *arrays):
    count = len(arrays)
    chans = conv_weight.shape[2]
    size = sum(a.size * a.dtype.itemsize for a in arrays)
    shapes = [jax.ShapeDtypeStruct(a.shape, a.dtype) for a in arrays]
    shapes.append(jax.ShapeDtypeStruct((EARLY,) + conv_weight.shape[1:], conv_weight.dtype))
    shapes.append(jax.ShapeDtypeStruct((chans, LANES), BF16))
    shapes.append(jax.ShapeDtypeStruct((LANES, chans), BF16))
    return pl.pallas_call(
        functools.partial(fetch_kernel, count),
        out_shape=tuple(shapes),
        in_specs=[VMEM] * count + [pl.BlockSpec(memory_space=pl.ANY)],
        out_specs=(VMEM,) * (count + 3),
        scratch_shapes=[pltpu.SemaphoreType.DMA],
        compiler_params=params(44),
        cost_estimate=cost(0, 2 * size),
        name="fetch",
    )(*arrays, conv_weight)


def cost(flops, moved):
    return pl.CostEstimate(flops=int(flops), bytes_accessed=int(moved), transcendentals=0)


def exchange(blocks):
    return lax.all_to_all(blocks, "frames", split_axis=0, concat_axis=0, tiled=True)


def body(
    skip, control, zero_weight, gn_gain, gn_bias, conv_weight, ln_gain, qkv_weight, out_weight
):
    f_dev, pixels, chans = skip.shape
    devices = lax.axis_size("frames")
    frame_count, per_dev, _ = control.shape
    rows = frame_count * per_dev
    own_control = exchange(control.reshape(rows, chans)).reshape(devices, f_dev, per_dev, chans)
    gains = jnp.stack((gn_gain, gn_bias, ln_gain))
    skip, zero_weight, gains, first_taps, gather, spread = fetch(
        conv_weight, skip, zero_weight, gains
    )
    first_frame = lax.axis_index("frames") * f_dev if frame_count > CLIP else jnp.int32(0)
    joined, stats = [], []
    for f in range(f_dev):
        frame_joined, frame_stats = pl.pallas_call(
            join_kernel,
            out_shape=(
                jax.ShapeDtypeStruct((pixels, chans), F32),
                jax.ShapeDtypeStruct((devices, LANES), F32),
            ),
            in_specs=[VMEM] * 5,
            out_specs=(VMEM, VMEM),
            compiler_params=params(8),
            cost_estimate=cost(2 * pixels * chans * chans, 32e6),
            name="join",
        )(skip[f], own_control[:, f].reshape(pixels, chans), zero_weight, gather, spread)
        joined.append(frame_joined)
        stats.append(frame_stats)
    all_stats = exchange(jnp.stack(stats, axis=1).reshape(devices * f_dev, LANES))
    resid, sent = [], []
    for f in range(f_dev):
        frame_resid, frame_sent = pl.pallas_call(
            conv_kernel,
            out_shape=(
                jax.ShapeDtypeStruct((pixels, chans), F32),
                jax.ShapeDtypeStruct((pixels, chans), BF16),
            ),
            in_specs=[SMEM] + [VMEM] * 5 + [pl.BlockSpec(memory_space=pl.ANY)],
            out_specs=(VMEM, VMEM),
            scratch_shapes=[
                pltpu.VMEM((pixels + 2 * W, 3 * chans), BF16),
                pltpu.VMEM((9 - EARLY, chans, chans), BF16),
                pltpu.SemaphoreType.DMA((9 - EARLY,)),
            ],
            compiler_params=params(50),
            cost_estimate=cost(18 * pixels * chans * chans, 9e6),
            name="conv",
        )(
            ((first_frame + f) // CLIP).reshape(1),
            joined[f],
            all_stats,
            spread,
            gains,
            first_taps,
            conv_weight,
        )
        resid.append(frame_resid)
        sent.append(frame_sent)
    by_pixel = jnp.stack(sent).reshape(f_dev, devices, per_dev, chans)
    by_pixel = exchange(by_pixel.transpose(1, 0, 2, 3).reshape(rows, chans))
    result = pl.pallas_call(
        functools.partial(attend_kernel, per_dev),
        out_shape=jax.ShapeDtypeStruct((rows, chans), BF16),
        in_specs=[VMEM] * 4,
        out_specs=VMEM,
        scratch_shapes=[pltpu.VMEM((rows, 3 * chans), BF16), pltpu.VMEM((rows, chans), BF16)],
        compiler_params=params(14),
        cost_estimate=cost(8 * rows * chans * chans, 4e6),
        name="attend",
    )(by_pixel, gains, qkv_weight, out_weight)
    mixed = exchange(result).reshape(devices, f_dev, per_dev, chans)
    mixed = mixed.transpose(1, 0, 2, 3).reshape(f_dev, pixels, chans)
    return (jnp.stack(resid) + mixed.astype(F32)).astype(BF16)


def solution(mesh):
    in_specs = (
        P(("groups", "frames"), None, None),
        P("groups", "frames", None),
        P(),
        P(),
        P(),
        P(),
        P(),
        P(),
        P(),
    )
    out_specs = P(("groups", "frames"), None, None)
    return jax.shard_map(body, mesh=mesh, in_specs=in_specs, out_specs=out_specs, check_vma=False)
```

```python
import functools
import math

import jax
import jax.numpy as jnp
from jax import lax
from jax.experimental import pallas as pl
from jax.experimental.pallas import tpu as pltpu
from jax.sharding import PartitionSpec as P

HEADS = 10
HD = 64
GROUPS = 32
CLIP = 32
W = 32
LANES = 128
EARLY = 2
COUNTS = (2, 1, 3, 3)

norm_epsilon = 1e-05
F32 = jnp.float32
BF16 = jnp.bfloat16
VMEM = pl.BlockSpec(memory_space=pltpu.VMEM)
SMEM = pl.BlockSpec(memory_space=pltpu.SMEM)


def params(mib):
    return pltpu.CompilerParams(
        vmem_limit_bytes=int(mib * 1024 * 1024)
    )


def member_dot(left, members):
    rows = left.shape[0]
    parts, rest = [], left
    for _ in range(3):
        part = rest.astype(BF16)
        parts.append(part.astype(F32))
        rest = rest - parts[-1]
    stacked = jnp.concatenate(parts).astype(BF16)
    product = jnp.dot(stacked, members, preferred_element_type=F32)
    return product[:rows] + product[rows : 2 * rows] + product[2 * rows :]


def group_members(chans, axis):
    size = chans // GROUPS
    first = lax.rem(lax.broadcasted_iota(jnp.int32, (LANES, LANES), 1 - axis), GROUPS) * size
    inner = lax.broadcasted_iota(jnp.int32, (LANES, LANES), axis) - first
    blocks = []
    for start in range(0, chans, LANES):
        place = inner + start
        blocks.append(jnp.where((place >= 0) & (place < size), 1.0, 0.0).astype(BF16))
    return jnp.concatenate(blocks, axis=axis)


def join_kernel(
    skip_ref, control_ref, weight_ref, gather_ref, spread_ref, joined_ref, stats_ref
):
    pixels, chans = skip_ref.shape
    zero_out = jnp.dot(control_ref[...], weight_ref[...], preferred_element_type=F32).astype(BF16)
    joined = skip_ref[...].astype(F32) + zero_out.astype(F32)
    joined_ref[...] = joined
    members = gather_ref[...]
    sums = jnp.broadcast_to(jnp.sum(joined, axis=0, keepdims=True), (8, chans))
    group_sums = member_dot(sums, members)
    lane_id = lax.broadcasted_iota(jnp.int32, (8, LANES), 1)
    group_mean = jnp.where(lane_id < GROUPS, group_sums, 0.0)
    group_mean = group_mean * (1.0 / (pixels * (chans // GROUPS)))
    chan_mean = member_dot(group_mean, spread_ref[...])[:1]
    spread = jnp.sum(jnp.square(joined_ref[...] - chan_mean), axis=0, keepdims=True)
    group_spread = member_dot(jnp.broadcast_to(spread, (8, chans)), members)
    stats = jnp.where(lane_id < GROUPS, group_sums, group_spread)
    stats = jnp.where(lane_id < 2 * GROUPS, stats, 0.0)
    stats_ref[...] = jnp.broadcast_to(stats[:1], stats_ref.shape)


def conv_kernel(
    clip_ref, joined_ref, stats_ref, spread_ref, gains_ref, first_ref, weight_hbm, resid_ref,
    sent_ref, window_ref, weight_ref, sems,
):
    copies = [
        pltpu.make_async_copy(weight_hbm.at[tap + EARLY], weight_ref.at[tap], sems.at[tap])
        for tap in range(9 - EARLY)
    ]
    for copy in copies:
        copy.start()
    pixels, chans = joined_ref.shape
    frames = stats_ref.shape[0]
    per_frame = float(pixels * (chans // GROUPS))
    stats = stats_ref[...]
    if frames > CLIP:
        row = lax.broadcasted_iota(jnp.int32, (frames, LANES), 0)
        first = clip_ref[0] * CLIP
        member = (row >= first) & (row < first + CLIP)
    else:
        member = jnp.full((frames, LANES), True)
    stats = jnp.where(member, stats, 0.0)
    mean_rows = stats * (1.0 / per_frame)
    lane_mean = jnp.sum(mean_rows, axis=0, keepdims=True) * (1.0 / CLIP)
    between = jnp.where(member, jnp.square(mean_rows - lane_mean), 0.0)
    lane_between = jnp.sum(between, axis=0, keepdims=True) * (1.0 / CLIP)
    lane_id = lax.broadcasted_iota(jnp.int32, (8, LANES), 1)
    row_id = lax.broadcasted_iota(jnp.int32, (8, LANES), 0)
    lane_var = jnp.where(lane_id < GROUPS, lane_between, lane_mean)
    lane_mean = jnp.where(lane_id < GROUPS, lane_mean, 0.0)
    chan_stats = member_dot(
        jnp.where(row_id == 0, lane_mean, lane_var), spread_ref[...]
    )
    chan_mean, chan_var = chan_stats[:1], chan_stats[1:2]
    edge = jnp.zeros((W, 3 * chans), BF16)
    window_ref[:W] = edge
    window_ref[W + pixels :] = edge
    factor = lax.rsqrt(chan_var + norm_epsilon)
    gain, bias = gains_ref[:1], gains_ref[1:2]
    col = lax.broadcasted_iota(jnp.int32, (W, chans), 0)

    @pl.loop(0, pixels // W)
    def _(line):
        here = pl.ds(pl.multiple_of(line * W, W), W)
        there = pl.ds(pl.multiple_of(line * W + W, W), W)
        activated = jax.nn.silu((joined_ref[here] - chan_mean) * factor * gain + bias)
        left = jnp.where(col == 0, 0.0, pltpu.roll(activated, 1, 0))
        right = jnp.where(col == W - 1, 0.0, pltpu.roll(activated, W - 1, 0))
        window_ref[there, :chans] = left.astype(BF16)
        window_ref[there, chans : 2 * chans] = activated.astype(BF16)
        window_ref[there, 2 * chans :] = right.astype(BF16)

    total = joined_ref[...]
    tap = 0
    for count in COUNTS:
        if tap == 0:
            weights = first_ref[...]
        else:
            taps = slice(tap - EARLY, tap - EARLY + count)
            for copy in copies[taps]:
                copy.wait()
            weights = weight_ref[taps]
        row = tap // 3 * W
        start = tap % 3 * chans
        total = total + jnp.dot(
            window_ref[row : row + pixels, start : start + count * chans],
            weights.reshape(count * chans, chans),
            preferred_element_type=F32,
        )
        tap += count
    resid_ref[...] = total
    sent_ref[...] = total.astype(BF16)


def moved_rows(rows, per_dev, groups):
    size = per_dev // groups
    old = lax.broadcasted_iota(jnp.int32, (1, rows), 1)
    frame, pixel = lax.div(old, per_dev), lax.rem(old, per_dev)
    part = lax.div(frame, CLIP) * groups + lax.div(pixel, size)
    return (part * CLIP + lax.rem(frame, CLIP)) * size + lax.rem(pixel, size)


def source_rows(rows, per_dev, groups):
    size = per_dev // groups
    new = lax.broadcasted_iota(jnp.int32, (1, rows), 1)
    part = lax.div(new, CLIP * size)
    frame = lax.div(part, groups) * CLIP + lax.rem(lax.div(new, size), CLIP)
    return frame * per_dev + lax.rem(part, groups) * size + lax.rem(new, size)


def select_rows(places, values):
    rows = values.shape[0]
    row = lax.broadcasted_iota(jnp.int32, (rows, rows), 0)
    return jnp.dot(
        jnp.where(row == places, 1.0, 0.0).astype(BF16), values, preferred_element_type=F32
    )


def attend_kernel(
    per_dev, resid_ref, gains_ref, qkv_ref, out_hbm, result_ref, rows_ref, mixed_ref, out_ref, sem
):
    copy = pltpu.make_async_copy(out_hbm, out_ref, sem)
    copy.start()
    rows, chans = resid_ref.shape
    groups = max(1, per_dev * CLIP // LANES)
    size = per_dev // groups
    resid = resid_ref[...]
    if groups > 1:
        resid = select_rows(moved_rows(rows, per_dev, groups), resid)
    else:
        resid = resid.astype(F32)
    mean = jnp.mean(resid, axis=-1, keepdims=True)
    centred = resid - mean
    var = jnp.mean(jnp.square(centred), axis=-1, keepdims=True)
    normed = (centred * lax.rsqrt(var + norm_epsilon) * gains_ref[2:3]).astype(BF16)
    rows_ref[...] = jnp.dot(normed, qkv_ref[...], preferred_element_type=F32).astype(BF16)
    scale = math.log2(math.e) / math.sqrt(HD)
    part_rows = size * CLIP
    period = max(size, 8)
    pixel = lax.rem(lax.broadcasted_iota(jnp.int32, (1, period, part_rows), 1), size)
    other = lax.rem(lax.broadcasted_iota(jnp.int32, (1, period, part_rows), 2), size)
    paired = pixel == other
    low_lanes = lax.broadcasted_iota(jnp.int32, (part_rows, LANES), 1) < HD
    one = jnp.ones((part_rows, LANES), BF16)
    zero = jnp.zeros((part_rows, LANES), BF16)

    def lanes_of(part, block, which):
        start = block * LANES + which * chans
        return rows_ref[part * part_rows : (part + 1) * part_rows, start : start + LANES]

    def scores_of(part, block):
        queries = lanes_of(part, block, 0)
        pair_queries = jnp.concatenate(
            [jnp.where(low_lanes, queries, zero), jnp.where(low_lanes, zero, queries)]
        )
        return lax.dot_general(
            pair_queries,
            lanes_of(part, block, 1),
            (((1,), (1,)), ((), ())),
            preferred_element_type=F32,
        )

    def weights_of(scores):
        scores = scores.reshape(2 * part_rows // period, period, part_rows)
        scores = jnp.where(paired, scores, -1e30)
        top = jnp.max(scores, axis=-1, keepdims=True)
        expon = jnp.exp2((scores - top) * scale)
        return expon.reshape(2 * part_rows, part_rows).astype(BF16)

    def mix(part, block, weights):
        values = lanes_of(part, block, 2)
        low = jnp.dot(
            weights[:part_rows], jnp.where(low_lanes, values, one), preferred_element_type=F32
        )
        high = jnp.dot(
            weights[part_rows:], jnp.where(low_lanes, one, values), preferred_element_type=F32
        )
        total = pltpu.roll(jnp.where(low_lanes, high, low), HD, 1)
        mixed = jnp.where(low_lanes, low, high) / total
        mixed_ref[
            part * part_rows : (part + 1) * part_rows, block * LANES : (block + 1) * LANES
        ] = mixed.astype(BF16)

    units = [
        (part, block) for part in range(rows // part_rows) for block in range(chans // LANES)
    ]
    for unit in units:
        mix(*unit, weights_of(scores_of(*unit)))
    mixed = mixed_ref[...]
    if groups > 1:
        mixed = select_rows(source_rows(rows, per_dev, groups), mixed).astype(BF16)
    copy.wait()
    result = jnp.dot(mixed, out_ref[...], preferred_element_type=F32)
    result_ref[...] = result.astype(BF16)


def fetch_kernel(count, *refs):
    taps_hbm = refs[count]
    taps_ref, gather_ref, spread_ref, sem = refs[-4:]
    copy = pltpu.make_async_copy(taps_hbm.at[pl.ds(0, EARLY)], taps_ref, sem)
    copy.start()
    for i in range(count):
        refs[count + 1 + i][...] = refs[i][...]
    gather_ref[...] = group_members(gather_ref.shape[0], 0)
    spread_ref[...] = group_members(spread_ref.shape[1], 1)
    copy.wait()


def fetch(conv_weight, *arrays):
    count = len(arrays)
    chans = conv_weight.shape[2]
    size = sum(a.size * a.dtype.itemsize for a in arrays)
    shapes = [jax.ShapeDtypeStruct(a.shape, a.dtype) for a in arrays]
    shapes.append(jax.ShapeDtypeStruct((EARLY,) + conv_weight.shape[1:], conv_weight.dtype))
    shapes.append(jax.ShapeDtypeStruct((chans, LANES), BF16))
    shapes.append(jax.ShapeDtypeStruct((LANES, chans), BF16))
    return pl.pallas_call(
        functools.partial(fetch_kernel, count),
        out_shape=tuple(shapes),
        in_specs=[VMEM] * count + [pl.BlockSpec(memory_space=pl.ANY)],
        out_specs=(VMEM,) * (count + 3),
        scratch_shapes=[pltpu.SemaphoreType.DMA],
        compiler_params=params(44),
        cost_estimate=cost(0, 2 * size),
        name="fetch",
    )(*arrays, conv_weight)


def late_kernel(array_hbm, after_hbm, array_ref, sem):
    copy = pltpu.make_async_copy(array_hbm, array_ref, sem)
    copy.start()
    copy.wait()


def fetch_late(array, after):
    return pl.pallas_call(
        late_kernel,
        out_shape=jax.ShapeDtypeStruct(array.shape, array.dtype),
        in_specs=[pl.BlockSpec(memory_space=pl.ANY)] * 2,
        out_specs=VMEM,
        scratch_shapes=[pltpu.SemaphoreType.DMA],
        compiler_params=params(53),
        cost_estimate=cost(0, 5e6),
        name="late",
    )(array, after)


def cost(flops, moved):
    return pl.CostEstimate(flops=int(flops), bytes_accessed=int(moved), transcendentals=0)


def exchange(blocks):
    return lax.all_to_all(blocks, "frames", split_axis=0, concat_axis=0, tiled=True)


def body(
    skip, control, zero_weight, gn_gain, gn_bias, conv_weight, ln_gain, qkv_weight, out_weight
):
    f_dev, pixels, chans = skip.shape
    devices = lax.axis_size("frames")
    frame_count, per_dev, _ = control.shape
    rows = frame_count * per_dev
    own_control = exchange(control.reshape(rows, chans)).reshape(devices, f_dev, per_dev, chans)
    gains = jnp.stack((gn_gain, gn_bias, ln_gain))
    skip, zero_weight, gains, first_taps, gather, spread = fetch(
        conv_weight, skip, zero_weight, gains
    )
    first_frame = lax.axis_index("frames") * f_dev if frame_count > CLIP else jnp.int32(0)
    joined, stats = [], []
    for f in range(f_dev):
        frame_joined, frame_stats = pl.pallas_call(
            join_kernel,
            out_shape=(
                jax.ShapeDtypeStruct((pixels, chans), F32),
                jax.ShapeDtypeStruct((devices, LANES), F32),
            ),
            in_specs=[VMEM] * 5,
            out_specs=(VMEM, VMEM),
            compiler_params=params(8),
            cost_estimate=cost(2 * pixels * chans * chans, 32e6),
            name="join",
        )(skip[f], own_control[:, f].reshape(pixels, chans), zero_weight, gather, spread)
        joined.append(frame_joined)
        stats.append(frame_stats)
    all_stats = exchange(jnp.stack(stats, axis=1).reshape(devices * f_dev, LANES))
    resid, sent = [], []
    for f in range(f_dev):
        frame_resid, frame_sent = pl.pallas_call(
            conv_kernel,
            out_shape=(
                jax.ShapeDtypeStruct((pixels, chans), F32),
                jax.ShapeDtypeStruct((pixels, chans), BF16),
            ),
            in_specs=[SMEM] + [VMEM] * 5 + [pl.BlockSpec(memory_space=pl.ANY)],
            out_specs=(VMEM, VMEM),
            scratch_shapes=[
                pltpu.VMEM((pixels + 2 * W, 3 * chans), BF16),
                pltpu.VMEM((9 - EARLY, chans, chans), BF16),
                pltpu.SemaphoreType.DMA((9 - EARLY,)),
            ],
            compiler_params=params(50),
            cost_estimate=cost(18 * pixels * chans * chans, 9e6),
            name="conv",
        )(
            ((first_frame + f) // CLIP).reshape(1),
            joined[f],
            all_stats,
            spread,
            gains,
            first_taps,
            conv_weight,
        )
        resid.append(frame_resid)
        sent.append(frame_sent)
    qkv_weight = fetch_late(qkv_weight, sent[0])
    by_pixel = jnp.stack(sent).reshape(f_dev, devices, per_dev, chans)
    by_pixel = exchange(by_pixel.transpose(1, 0, 2, 3).reshape(rows, chans))
    result = pl.pallas_call(
        functools.partial(attend_kernel, per_dev),
        out_shape=jax.ShapeDtypeStruct((rows, chans), BF16),
        in_specs=[VMEM] * 3 + [pl.BlockSpec(memory_space=pl.ANY)],
        out_specs=VMEM,
        scratch_shapes=[
            pltpu.VMEM((rows, 3 * chans), BF16),
            pltpu.VMEM((rows, chans), BF16),
            pltpu.VMEM(out_weight.shape, BF16),
            pltpu.SemaphoreType.DMA,
        ],
        compiler_params=params(53),
        cost_estimate=cost(8 * rows * chans * chans, 4e6),
        name="attend",
    )(by_pixel, gains, qkv_weight, out_weight)
    mixed = exchange(result).reshape(devices, f_dev, per_dev, chans)
    mixed = mixed.transpose(1, 0, 2, 3).reshape(f_dev, pixels, chans)
    return (jnp.stack(resid) + mixed.astype(F32)).astype(BF16)


def solution(mesh):
    in_specs = (
        P(("groups", "frames"), None, None),
        P("groups", "frames", None),
        P(),
        P(),
        P(),
        P(),
        P(),
        P(),
        P(),
    )
    out_specs = P(("groups", "frames"), None, None)
    return jax.shard_map(body, mesh=mesh, in_specs=in_specs, out_specs=out_specs, check_vma=False)
```

```python
import functools
import math

import jax
import jax.numpy as jnp
from jax import lax
from jax.experimental import pallas as pl
from jax.experimental.pallas import tpu as pltpu
from jax.sharding import PartitionSpec as P

HEADS = 10
HD = 64
GROUPS = 32
CLIP = 32
W = 32
LANES = 128
EARLY = 2
COUNTS = (2, 1, 3, 3)

norm_epsilon = 1e-05
F32 = jnp.float32
BF16 = jnp.bfloat16
VMEM = pl.BlockSpec(memory_space=pltpu.VMEM)
SMEM = pl.BlockSpec(memory_space=pltpu.SMEM)


def params(mib):
    return pltpu.CompilerParams(
        vmem_limit_bytes=mib * 1024 * 1024
    )


def member_dot(left, members):
    rows = left.shape[0]
    parts, rest = [], left
    for _ in range(3):
        part = rest.astype(BF16)
        parts.append(part.astype(F32))
        rest = rest - parts[-1]
    stacked = jnp.concatenate(parts).astype(BF16)
    product = jnp.dot(stacked, members, preferred_element_type=F32)
    return product[:rows] + product[rows : 2 * rows] + product[2 * rows :]


def group_members(chans, axis):
    size = chans // GROUPS
    first = lax.rem(lax.broadcasted_iota(jnp.int32, (LANES, LANES), 1 - axis), GROUPS) * size
    inner = lax.broadcasted_iota(jnp.int32, (LANES, LANES), axis) - first
    blocks = []
    for start in range(0, chans, LANES):
        place = inner + start
        blocks.append(jnp.where((place >= 0) & (place < size), 1.0, 0.0).astype(BF16))
    return jnp.concatenate(blocks, axis=axis)


def join_kernel(
    skip_ref, control_ref, weight_ref, gather_ref, spread_ref, joined_ref, stats_ref
):
    pixels, chans = skip_ref.shape
    zero_out = jnp.dot(control_ref[...], weight_ref[...], preferred_element_type=F32).astype(BF16)
    joined = skip_ref[...].astype(F32) + zero_out.astype(F32)
    joined_ref[...] = joined
    members = gather_ref[...]
    sums = jnp.broadcast_to(jnp.sum(joined, axis=0, keepdims=True), (8, chans))
    group_sums = member_dot(sums, members)
    lane_id = lax.broadcasted_iota(jnp.int32, (8, LANES), 1)
    group_mean = jnp.where(lane_id < GROUPS, group_sums, 0.0)
    group_mean = group_mean * (1.0 / (pixels * (chans // GROUPS)))
    chan_mean = member_dot(group_mean, spread_ref[...])[:1]
    spread = jnp.sum(jnp.square(joined_ref[...] - chan_mean), axis=0, keepdims=True)
    group_spread = member_dot(jnp.broadcast_to(spread, (8, chans)), members)
    stats = jnp.where(lane_id < GROUPS, group_sums, group_spread)
    stats = jnp.where(lane_id < 2 * GROUPS, stats, 0.0)
    stats_ref[...] = jnp.broadcast_to(stats[:1], stats_ref.shape)


def conv_kernel(
    clip_ref, joined_ref, stats_ref, spread_ref, gains_ref, first_ref, weight_hbm, resid_ref,
    sent_ref, window_ref, weight_ref, sems,
):
    copies = [
        pltpu.make_async_copy(weight_hbm.at[tap + EARLY], weight_ref.at[tap], sems.at[tap])
        for tap in range(9 - EARLY)
    ]
    for copy in copies:
        copy.start()
    pixels, chans = joined_ref.shape
    frames = stats_ref.shape[0]
    per_frame = float(pixels * (chans // GROUPS))
    stats = stats_ref[...]
    if frames > CLIP:
        row = lax.broadcasted_iota(jnp.int32, (frames, LANES), 0)
        first = clip_ref[0] * CLIP
        member = (row >= first) & (row < first + CLIP)
    else:
        member = jnp.full((frames, LANES), True)
    stats = jnp.where(member, stats, 0.0)
    mean_rows = stats * (1.0 / per_frame)
    lane_mean = jnp.sum(mean_rows, axis=0, keepdims=True) * (1.0 / CLIP)
    between = jnp.where(member, jnp.square(mean_rows - lane_mean), 0.0)
    lane_between = jnp.sum(between, axis=0, keepdims=True) * (1.0 / CLIP)
    lane_id = lax.broadcasted_iota(jnp.int32, (8, LANES), 1)
    row_id = lax.broadcasted_iota(jnp.int32, (8, LANES), 0)
    lane_var = jnp.where(lane_id < GROUPS, lane_between, lane_mean)
    lane_mean = jnp.where(lane_id < GROUPS, lane_mean, 0.0)
    chan_stats = member_dot(
        jnp.where(row_id == 0, lane_mean, lane_var), spread_ref[...]
    )
    chan_mean, chan_var = chan_stats[:1], chan_stats[1:2]
    edge = jnp.zeros((W, 3 * chans), BF16)
    window_ref[:W] = edge
    window_ref[W + pixels :] = edge
    factor = lax.rsqrt(chan_var + norm_epsilon)
    gain, bias = gains_ref[:1], gains_ref[1:2]
    col = lax.broadcasted_iota(jnp.int32, (W, chans), 0)

    @pl.loop(0, pixels // W)
    def _(line):
        here = pl.ds(pl.multiple_of(line * W, W), W)
        there = pl.ds(pl.multiple_of(line * W + W, W), W)
        activated = jax.nn.silu((joined_ref[here] - chan_mean) * factor * gain + bias)
        left = jnp.where(col == 0, 0.0, pltpu.roll(activated, 1, 0))
        right = jnp.where(col == W - 1, 0.0, pltpu.roll(activated, W - 1, 0))
        window_ref[there, :chans] = left.astype(BF16)
        window_ref[there, chans : 2 * chans] = activated.astype(BF16)
        window_ref[there, 2 * chans :] = right.astype(BF16)

    total = joined_ref[...]
    tap = waited = 0
    for count in COUNTS:
        if tap == 0:
            weights = first_ref[...]
        else:
            taps = slice(tap - EARLY, tap - EARLY + count)
            due = 6 - EARLY if tap < 6 else 9 - EARLY
            while waited < due:
                copies[waited].wait()
                waited += 1
            weights = weight_ref[taps]
        row = tap // 3 * W
        start = tap % 3 * chans
        total = total + jnp.dot(
            window_ref[row : row + pixels, start : start + count * chans],
            weights.reshape(count * chans, chans),
            preferred_element_type=F32,
        )
        tap += count
    resid_ref[...] = total
    sent_ref[...] = total.astype(BF16)


def moved_rows(rows, per_dev, groups):
    size = per_dev // groups
    old = lax.broadcasted_iota(jnp.int32, (1, rows), 1)
    frame, pixel = lax.div(old, per_dev), lax.rem(old, per_dev)
    part = lax.div(frame, CLIP) * groups + lax.div(pixel, size)
    return (part * CLIP + lax.rem(frame, CLIP)) * size + lax.rem(pixel, size)


def source_rows(rows, per_dev, groups):
    size = per_dev // groups
    new = lax.broadcasted_iota(jnp.int32, (1, rows), 1)
    part = lax.div(new, CLIP * size)
    frame = lax.div(part, groups) * CLIP + lax.rem(lax.div(new, size), CLIP)
    return frame * per_dev + lax.rem(part, groups) * size + lax.rem(new, size)


def select_rows(places, values):
    rows = values.shape[0]
    row = lax.broadcasted_iota(jnp.int32, (rows, rows), 0)
    return jnp.dot(
        jnp.where(row == places, 1.0, 0.0).astype(BF16), values, preferred_element_type=F32
    )


def attend_kernel(
    per_dev, resid_ref, gains_ref, qkv_ref, out_ref, result_ref, rows_ref, mixed_ref
):
    rows, chans = resid_ref.shape
    groups = max(1, per_dev * CLIP // LANES)
    size = per_dev // groups
    resid = resid_ref[...]
    if groups > 1:
        resid = select_rows(moved_rows(rows, per_dev, groups), resid)
    else:
        resid = resid.astype(F32)
    mean = jnp.mean(resid, axis=-1, keepdims=True)
    centred = resid - mean
    var = jnp.mean(jnp.square(centred), axis=-1, keepdims=True)
    normed = (centred * lax.rsqrt(var + norm_epsilon) * gains_ref[2:3]).astype(BF16)
    rows_ref[...] = jnp.dot(normed, qkv_ref[...], preferred_element_type=F32).astype(BF16)
    scale = math.log2(math.e) / math.sqrt(HD)
    part_rows = size * CLIP
    period = max(size, 8)
    pixel = lax.rem(lax.broadcasted_iota(jnp.int32, (1, period, part_rows), 1), size)
    other = lax.rem(lax.broadcasted_iota(jnp.int32, (1, period, part_rows), 2), size)
    paired = pixel == other
    low_lanes = lax.broadcasted_iota(jnp.int32, (part_rows, LANES), 1) < HD
    one = jnp.ones((part_rows, LANES), BF16)
    zero = jnp.zeros((part_rows, LANES), BF16)

    def lanes_of(part, block, which):
        start = block * LANES + which * chans
        return rows_ref[part * part_rows : (part + 1) * part_rows, start : start + LANES]

    def scores_of(part, block):
        queries = lanes_of(part, block, 0)
        pair_queries = jnp.concatenate(
            [jnp.where(low_lanes, queries, zero), jnp.where(low_lanes, zero, queries)]
        )
        return lax.dot_general(
            pair_queries,
            lanes_of(part, block, 1),
            (((1,), (1,)), ((), ())),
            preferred_element_type=F32,
        )

    def weights_of(scores):
        scores = scores.reshape(2 * part_rows // period, period, part_rows)
        scores = jnp.where(paired, scores, -1e30)
        top = jnp.max(scores, axis=-1, keepdims=True)
        expon = jnp.exp2((scores - top) * scale)
        return expon.reshape(2 * part_rows, part_rows).astype(BF16)

    def mix(part, block, weights):
        values = lanes_of(part, block, 2)
        low = jnp.dot(
            weights[:part_rows], jnp.where(low_lanes, values, one), preferred_element_type=F32
        )
        high = jnp.dot(
            weights[part_rows:], jnp.where(low_lanes, one, values), preferred_element_type=F32
        )
        total = pltpu.roll(jnp.where(low_lanes, high, low), HD, 1)
        mixed = jnp.where(low_lanes, low, high) / total
        mixed_ref[
            part * part_rows : (part + 1) * part_rows, block * LANES : (block + 1) * LANES
        ] = mixed.astype(BF16)

    units = [
        (part, block) for part in range(rows // part_rows) for block in range(chans // LANES)
    ]
    for unit in units:
        mix(*unit, weights_of(scores_of(*unit)))
    mixed = mixed_ref[...]
    if groups > 1:
        mixed = select_rows(source_rows(rows, per_dev, groups), mixed).astype(BF16)
    result = jnp.dot(mixed, out_ref[...], preferred_element_type=F32)
    result_ref[...] = result.astype(BF16)


def fetch_kernel(count, *refs):
    taps_hbm = refs[count]
    taps_ref, gather_ref, spread_ref, sem = refs[-4:]
    copy = pltpu.make_async_copy(taps_hbm.at[pl.ds(0, EARLY)], taps_ref, sem)
    copy.start()
    for i in range(count):
        refs[count + 1 + i][...] = refs[i][...]
    gather_ref[...] = group_members(gather_ref.shape[0], 0)
    spread_ref[...] = group_members(spread_ref.shape[1], 1)
    copy.wait()


def fetch(conv_weight, *arrays):
    count = len(arrays)
    chans = conv_weight.shape[2]
    size = sum(a.size * a.dtype.itemsize for a in arrays)
    shapes = [jax.ShapeDtypeStruct(a.shape, a.dtype) for a in arrays]
    shapes.append(jax.ShapeDtypeStruct((EARLY,) + conv_weight.shape[1:], conv_weight.dtype))
    shapes.append(jax.ShapeDtypeStruct((chans, LANES), BF16))
    shapes.append(jax.ShapeDtypeStruct((LANES, chans), BF16))
    return pl.pallas_call(
        functools.partial(fetch_kernel, count),
        out_shape=tuple(shapes),
        in_specs=[VMEM] * count + [pl.BlockSpec(memory_space=pl.ANY)],
        out_specs=(VMEM,) * (count + 3),
        scratch_shapes=[pltpu.SemaphoreType.DMA],
        compiler_params=params(44),
        cost_estimate=cost(0, 2 * size),
        name="fetch",
    )(*arrays, conv_weight)


def cost(flops, moved):
    return pl.CostEstimate(flops=int(flops), bytes_accessed=int(moved), transcendentals=0)


def exchange(blocks):
    return lax.all_to_all(blocks, "frames", split_axis=0, concat_axis=0, tiled=True)


def body(
    skip, control, zero_weight, gn_gain, gn_bias, conv_weight, ln_gain, qkv_weight, out_weight
):
    f_dev, pixels, chans = skip.shape
    devices = lax.axis_size("frames")
    frame_count, per_dev, _ = control.shape
    rows = frame_count * per_dev
    own_control = exchange(control.reshape(rows, chans)).reshape(devices, f_dev, per_dev, chans)
    gains = jnp.stack((gn_gain, gn_bias, ln_gain))
    skip, zero_weight, gains, first_taps, gather, spread = fetch(
        conv_weight, skip, zero_weight, gains
    )
    first_frame = lax.axis_index("frames") * f_dev if frame_count > CLIP else jnp.int32(0)
    joined, stats = [], []
    for f in range(f_dev):
        frame_joined, frame_stats = pl.pallas_call(
            join_kernel,
            out_shape=(
                jax.ShapeDtypeStruct((pixels, chans), F32),
                jax.ShapeDtypeStruct((devices, LANES), F32),
            ),
            in_specs=[VMEM] * 5,
            out_specs=(VMEM, VMEM),
            compiler_params=params(8),
            cost_estimate=cost(2 * pixels * chans * chans, 32e6),
            name="join",
        )(skip[f], own_control[:, f].reshape(pixels, chans), zero_weight, gather, spread)
        joined.append(frame_joined)
        stats.append(frame_stats)
    all_stats = exchange(jnp.stack(stats, axis=1).reshape(devices * f_dev, LANES))
    resid, sent = [], []
    for f in range(f_dev):
        frame_resid, frame_sent = pl.pallas_call(
            conv_kernel,
            out_shape=(
                jax.ShapeDtypeStruct((pixels, chans), F32),
                jax.ShapeDtypeStruct((pixels, chans), BF16),
            ),
            in_specs=[SMEM] + [VMEM] * 5 + [pl.BlockSpec(memory_space=pl.ANY)],
            out_specs=(VMEM, VMEM),
            scratch_shapes=[
                pltpu.VMEM((pixels + 2 * W, 3 * chans), BF16),
                pltpu.VMEM((9 - EARLY, chans, chans), BF16),
                pltpu.SemaphoreType.DMA((9 - EARLY,)),
            ],
            compiler_params=params(50),
            cost_estimate=cost(18 * pixels * chans * chans, 9e6),
            name="conv",
        )(
            ((first_frame + f) // CLIP).reshape(1),
            joined[f],
            all_stats,
            spread,
            gains,
            first_taps,
            conv_weight,
        )
        resid.append(frame_resid)
        sent.append(frame_sent)
    by_pixel = jnp.stack(sent).reshape(f_dev, devices, per_dev, chans)
    by_pixel = exchange(by_pixel.transpose(1, 0, 2, 3).reshape(rows, chans))
    result = pl.pallas_call(
        functools.partial(attend_kernel, per_dev),
        out_shape=jax.ShapeDtypeStruct((rows, chans), BF16),
        in_specs=[VMEM] * 4,
        out_specs=VMEM,
        scratch_shapes=[pltpu.VMEM((rows, 3 * chans), BF16), pltpu.VMEM((rows, chans), BF16)],
        compiler_params=params(14),
        cost_estimate=cost(8 * rows * chans * chans, 4e6),
        name="attend",
    )(by_pixel, gains, qkv_weight, out_weight)
    mixed = exchange(result).reshape(devices, f_dev, per_dev, chans)
    mixed = mixed.transpose(1, 0, 2, 3).reshape(f_dev, pixels, chans)
    return (jnp.stack(resid) + mixed.astype(F32)).astype(BF16)


def solution(mesh):
    in_specs = (
        P(("groups", "frames"), None, None),
        P("groups", "frames", None),
        P(),
        P(),
        P(),
        P(),
        P(),
        P(),
        P(),
    )
    out_specs = P(("groups", "frames"), None, None)
    return jax.shard_map(body, mesh=mesh, in_specs=in_specs, out_specs=out_specs, check_vma=False)
```

```python
import functools
import math

import jax
import jax.numpy as jnp
from jax import lax
from jax.experimental import pallas as pl
from jax.experimental.pallas import tpu as pltpu
from jax.sharding import PartitionSpec as P

HEADS = 10
HD = 64
GROUPS = 32
CLIP = 32
W = 32
LANES = 128
EARLY = 2
COUNTS = (2, 1, 3, 2, 1)

norm_epsilon = 1e-05
F32 = jnp.float32
BF16 = jnp.bfloat16
VMEM = pl.BlockSpec(memory_space=pltpu.VMEM)
SMEM = pl.BlockSpec(memory_space=pltpu.SMEM)


def params(mib):
    return pltpu.CompilerParams(vmem_limit_bytes=mib * 1024 * 1024)


def member_dot(left, members):
    rows = left.shape[0]
    parts, rest = [], left
    for _ in range(3):
        part = rest.astype(BF16)
        parts.append(part.astype(F32))
        rest = rest - parts[-1]
    stacked = jnp.concatenate(parts).astype(BF16)
    product = jnp.dot(stacked, members, preferred_element_type=F32)
    return product[:rows] + product[rows : 2 * rows] + product[2 * rows :]


def group_members(chans, axis):
    size = chans // GROUPS
    first = lax.rem(lax.broadcasted_iota(jnp.int32, (LANES, LANES), 1 - axis), GROUPS) * size
    inner = lax.broadcasted_iota(jnp.int32, (LANES, LANES), axis) - first
    blocks = []
    for start in range(0, chans, LANES):
        place = inner + start
        blocks.append(jnp.where((place >= 0) & (place < size), 1.0, 0.0).astype(BF16))
    return jnp.concatenate(blocks, axis=axis)


def join_kernel(skip_ref, control_ref, weight_ref, joined_ref, stats_ref):
    pixels, chans = skip_ref.shape
    zero_out = jnp.dot(control_ref[...], weight_ref[...], preferred_element_type=F32).astype(BF16)
    joined = skip_ref[...].astype(F32) + zero_out.astype(F32)
    joined_ref[...] = joined
    members = group_members(chans, 0)
    sums = jnp.broadcast_to(jnp.sum(joined, axis=0, keepdims=True), (8, chans))
    group_sums = member_dot(sums, members)
    lane_id = lax.broadcasted_iota(jnp.int32, (8, LANES), 1)
    group_mean = jnp.where(lane_id < GROUPS, group_sums, 0.0)
    group_mean = group_mean * (1.0 / (pixels * (chans // GROUPS)))
    chan_mean = member_dot(group_mean, group_members(chans, 1))[:1]
    spread = jnp.sum(jnp.square(joined_ref[...] - chan_mean), axis=0, keepdims=True)
    group_spread = member_dot(jnp.broadcast_to(spread, (8, chans)), members)
    stats = jnp.where(lane_id < GROUPS, group_sums, group_spread)
    stats = jnp.where(lane_id < 2 * GROUPS, stats, 0.0)
    stats_ref[...] = jnp.broadcast_to(stats[:1], stats_ref.shape)


def conv_kernel(
    clip_ref, joined_ref, stats_ref, gains_ref, first_ref, weight_hbm, resid_ref, sent_ref,
    window_ref, weight_ref, sems,
):
    copies = [
        pltpu.make_async_copy(weight_hbm.at[tap + EARLY], weight_ref.at[tap], sems.at[tap])
        for tap in range(9 - EARLY)
    ]
    for copy in copies:
        copy.start()
    pixels, chans = joined_ref.shape
    frames = stats_ref.shape[0]
    per_frame = float(pixels * (chans // GROUPS))
    stats = stats_ref[...]
    if frames > CLIP:
        row = lax.broadcasted_iota(jnp.int32, (frames, LANES), 0)
        first = clip_ref[0] * CLIP
        member = (row >= first) & (row < first + CLIP)
    else:
        member = jnp.full((frames, LANES), True)
    stats = jnp.where(member, stats, 0.0)
    mean_rows = stats * (1.0 / per_frame)
    lane_mean = jnp.sum(mean_rows, axis=0, keepdims=True) * (1.0 / CLIP)
    between = jnp.where(member, jnp.square(mean_rows - lane_mean), 0.0)
    lane_between = jnp.sum(between, axis=0, keepdims=True) * (1.0 / CLIP)
    lane_id = lax.broadcasted_iota(jnp.int32, (8, LANES), 1)
    row_id = lax.broadcasted_iota(jnp.int32, (8, LANES), 0)
    lane_var = jnp.where(lane_id < GROUPS, lane_between, lane_mean)
    lane_mean = jnp.where(lane_id < GROUPS, lane_mean, 0.0)
    chan_stats = member_dot(
        jnp.where(row_id == 0, lane_mean, lane_var), group_members(chans, 1)
    )
    chan_mean, chan_var = chan_stats[:1], chan_stats[1:2]
    edge = jnp.zeros((W, 3 * chans), BF16)
    window_ref[:W] = edge
    window_ref[W + pixels :] = edge
    factor = lax.rsqrt(chan_var + norm_epsilon)
    gain, bias = gains_ref[:1], gains_ref[1:2]
    col = lax.broadcasted_iota(jnp.int32, (W, chans), 0)

    @pl.loop(0, pixels // W)
    def _(line):
        here = pl.ds(pl.multiple_of(line * W, W), W)
        there = pl.ds(pl.multiple_of(line * W + W, W), W)
        activated = jax.nn.silu((joined_ref[here] - chan_mean) * factor * gain + bias)
        left = jnp.where(col == 0, 0.0, pltpu.roll(activated, 1, 0))
        right = jnp.where(col == W - 1, 0.0, pltpu.roll(activated, W - 1, 0))
        window_ref[there, :chans] = left.astype(BF16)
        window_ref[there, chans : 2 * chans] = activated.astype(BF16)
        window_ref[there, 2 * chans :] = right.astype(BF16)

    total = joined_ref[...]
    tap = 0
    for count in COUNTS:
        if tap == 0:
            weights = first_ref[...]
        else:
            taps = slice(tap - EARLY, tap - EARLY + count)
            for copy in copies[taps]:
                copy.wait()
            weights = weight_ref[taps]
        row = tap // 3 * W
        start = tap % 3 * chans
        total = total + jnp.dot(
            window_ref[row : row + pixels, start : start + count * chans],
            weights.reshape(count * chans, chans),
            preferred_element_type=F32,
        )
        tap += count
    resid_ref[...] = total
    sent_ref[...] = total.astype(BF16)


def attend_kernel(
    per_dev, resid_ref, gains_ref, qkv_ref, out_ref, result_ref, rows_ref, mixed_ref, scores_ref,
    weights_ref,
):
    rows, chans = resid_ref.shape
    resid = resid_ref[...].astype(F32)
    mean = jnp.mean(resid, axis=-1, keepdims=True)
    centred = resid - mean
    var = jnp.mean(jnp.square(centred), axis=-1, keepdims=True)
    normed = (centred * lax.rsqrt(var + norm_epsilon) * gains_ref[2:3]).astype(BF16)
    rows_ref[...] = jnp.dot(normed, qkv_ref[...], preferred_element_type=F32).astype(BF16)
    scale = math.log2(math.e) / math.sqrt(HD)
    clip_rows = per_dev * CLIP
    period = max(per_dev, 8)
    pixel = lax.rem(lax.broadcasted_iota(jnp.int32, (1, period, clip_rows), 1), per_dev)
    other = lax.rem(lax.broadcasted_iota(jnp.int32, (1, period, clip_rows), 2), per_dev)
    paired = pixel == other
    low_lanes = lax.broadcasted_iota(jnp.int32, (clip_rows, LANES), 1) < HD
    one = jnp.ones((clip_rows, LANES), BF16)
    zero = jnp.zeros((clip_rows, LANES), BF16)
    for first_row in range(0, rows, clip_rows):
        clip = slice(first_row, first_row + clip_rows)

        blocks = chans // LANES

        def lanes_of(block, part):
            start = block * LANES + part * chans
            return rows_ref[clip, start : start + LANES]

        def scores_of(block):
            queries = lanes_of(block, 0)
            pair_queries = jnp.concatenate(
                [jnp.where(low_lanes, queries, zero), jnp.where(low_lanes, zero, queries)]
            )
            scores_ref[block % 2] = lax.dot_general(
                pair_queries,
                lanes_of(block, 1),
                (((1,), (1,)), ((), ())),
                preferred_element_type=F32,
            )

        def weights_of(block):
            scores = scores_ref[block % 2].reshape(2 * clip_rows // period, period, clip_rows)
            scores = jnp.where(paired, scores, -1e30)
            top = jnp.max(scores, axis=-1, keepdims=True)
            expon = jnp.exp2((scores - top) * scale)
            weights_ref[block % 2] = expon.reshape(2 * clip_rows, clip_rows).astype(BF16)

        def mix(block):
            values = lanes_of(block, 2)
            weights = weights_ref[block % 2]
            low = jnp.dot(
                weights[:clip_rows], jnp.where(low_lanes, values, one), preferred_element_type=F32
            )
            high = jnp.dot(
                weights[clip_rows:], jnp.where(low_lanes, one, values), preferred_element_type=F32
            )
            total = pltpu.roll(jnp.where(low_lanes, high, low), HD, 1)
            mixed = jnp.where(low_lanes, low, high) / total
            mixed_ref[clip, block * LANES : (block + 1) * LANES] = mixed.astype(BF16)

        scores_of(0)
        for block in range(blocks):
            if block + 1 < blocks:
                scores_of(block + 1)
            weights_of(block)
            if block:
                mix(block - 1)
        mix(blocks - 1)
    result = jnp.dot(mixed_ref[...], out_ref[...], preferred_element_type=F32)
    result_ref[...] = result.astype(BF16)


def fetch_kernel(count, *refs):
    sem = refs[-1]
    taps_hbm, taps_ref = refs[count], refs[-2]
    copy = pltpu.make_async_copy(taps_hbm.at[pl.ds(0, EARLY)], taps_ref, sem)
    copy.start()
    for i in range(count):
        refs[count + 1 + i][...] = refs[i][...]
    copy.wait()


def fetch(conv_weight, *arrays):
    count = len(arrays)
    size = sum(a.size * a.dtype.itemsize for a in arrays)
    shapes = [jax.ShapeDtypeStruct(a.shape, a.dtype) for a in arrays]
    shapes.append(jax.ShapeDtypeStruct((EARLY,) + conv_weight.shape[1:], conv_weight.dtype))
    return pl.pallas_call(
        functools.partial(fetch_kernel, count),
        out_shape=tuple(shapes),
        in_specs=[VMEM] * count + [pl.BlockSpec(memory_space=pl.ANY)],
        out_specs=(VMEM,) * (count + 1),
        scratch_shapes=[pltpu.SemaphoreType.DMA],
        compiler_params=params(44),
        cost_estimate=cost(0, 2 * size),
        name="fetch",
    )(*arrays, conv_weight)


def cost(flops, moved):
    return pl.CostEstimate(flops=int(flops), bytes_accessed=int(moved), transcendentals=0)


def exchange(blocks):
    return lax.all_to_all(blocks, "frames", split_axis=0, concat_axis=0, tiled=True)


def body(
    skip, control, zero_weight, gn_gain, gn_bias, conv_weight, ln_gain, qkv_weight, out_weight
):
    f_dev, pixels, chans = skip.shape
    devices = lax.axis_size("frames")
    frame_count, per_dev, _ = control.shape
    rows = frame_count * per_dev
    own_control = exchange(control.reshape(rows, chans)).reshape(devices, f_dev, per_dev, chans)
    gains = jnp.stack((gn_gain, gn_bias, ln_gain))
    skip, zero_weight, gains, first_taps = fetch(conv_weight, skip, zero_weight, gains)
    first_frame = lax.axis_index("frames") * f_dev if frame_count > CLIP else jnp.int32(0)
    joined, stats = [], []
    for f in range(f_dev):
        frame_joined, frame_stats = pl.pallas_call(
            join_kernel,
            out_shape=(
                jax.ShapeDtypeStruct((pixels, chans), F32),
                jax.ShapeDtypeStruct((devices, LANES), F32),
            ),
            in_specs=[VMEM] * 3,
            out_specs=(VMEM, VMEM),
            compiler_params=params(8),
            cost_estimate=cost(2 * pixels * chans * chans, 32e6),
            name="join",
        )(skip[f], own_control[:, f].reshape(pixels, chans), zero_weight)
        joined.append(frame_joined)
        stats.append(frame_stats)
    all_stats = exchange(jnp.stack(stats, axis=1).reshape(devices * f_dev, LANES))
    resid, sent = [], []
    for f in range(f_dev):
        frame_resid, frame_sent = pl.pallas_call(
            conv_kernel,
            out_shape=(
                jax.ShapeDtypeStruct((pixels, chans), F32),
                jax.ShapeDtypeStruct((pixels, chans), BF16),
            ),
            in_specs=[SMEM] + [VMEM] * 4 + [pl.BlockSpec(memory_space=pl.ANY)],
            out_specs=(VMEM, VMEM),
            scratch_shapes=[
                pltpu.VMEM((pixels + 2 * W, 3 * chans), BF16),
                pltpu.VMEM((9 - EARLY, chans, chans), BF16),
                pltpu.SemaphoreType.DMA((9 - EARLY,)),
            ],
            compiler_params=params(50),
            cost_estimate=cost(18 * pixels * chans * chans, 9e6),
            name="conv",
        )(
            ((first_frame + f) // CLIP).reshape(1),
            joined[f],
            all_stats,
            gains,
            first_taps,
            conv_weight,
        )
        resid.append(frame_resid)
        sent.append(frame_sent)
    by_pixel = jnp.stack(sent).reshape(f_dev, devices, per_dev, chans)
    by_pixel = exchange(by_pixel.transpose(1, 0, 2, 3).reshape(rows, chans))
    result = pl.pallas_call(
        functools.partial(attend_kernel, per_dev),
        out_shape=jax.ShapeDtypeStruct((rows, chans), BF16),
        in_specs=[VMEM] * 4,
        out_specs=VMEM,
        scratch_shapes=[
            pltpu.VMEM((rows, 3 * chans), BF16),
            pltpu.VMEM((rows, chans), BF16),
            pltpu.VMEM((2, 2 * per_dev * CLIP, per_dev * CLIP), F32),
            pltpu.VMEM((2, 2 * per_dev * CLIP, per_dev * CLIP), BF16),
        ],
        compiler_params=params(14),
        cost_estimate=cost(8 * rows * chans * chans, 4e6),
        name="attend",
    )(by_pixel, gains, qkv_weight, out_weight)
    mixed = exchange(result).reshape(devices, f_dev, per_dev, chans)
    mixed = mixed.transpose(1, 0, 2, 3).reshape(f_dev, pixels, chans)
    return (jnp.stack(resid) + mixed.astype(F32)).astype(BF16)


def solution(mesh):
    in_specs = (
        P(("groups", "frames"), None, None),
        P("groups", "frames", None),
        P(),
        P(),
        P(),
        P(),
        P(),
        P(),
        P(),
    )
    out_specs = P(("groups", "frames"), None, None)
    return jax.shard_map(body, mesh=mesh, in_specs=in_specs, out_specs=out_specs, check_vma=False)
```
